32 devices in a mesh: dp: 8 (over z, y), shard: 4 (over x, core).
Axes of the slice: x: 2, y: 2, z: 4, core: 2. Of those that a mesh axis runs over, the one named last changes fastest.
Arguments:
- embedded: bfloat16 [30720, 1280], P(('dp', 'shard')), may hold values from -6 to 6
- mask_token_embedding: bfloat16 [1280], replicated, may hold values from -5 to 5
- destination: int32 [30720], P(('dp', 'shard')), may hold values from 0 to 8, as said below
- position: int32 [30720], P(('dp', 'shard')), may hold values from 0 to 79, as said below
- length: int32 [30720], P(('dp', 'shard')), may hold values from 0 to 80, as said below
- unmask_order: int32 [30720], P(('dp', 'shard')), may hold values from 0 to 79, as said below
- timestep: int32 [30720], P(('dp', 'shard')), may hold values from 0 to 80, as said below
- upstream: bfloat16 [12288, 1280], P(('dp', 'shard')), may hold values from -0.29882812 to 0.29882812
- gain_in: float32 [1280], replicated, may hold values from 0.4 to 1.6
- weight_in: bfloat16 [1280, 640], replicated, may hold values from -0.15625 to 0.15625
- gain_mid: float32 [640], replicated, may hold values from 0.4 to 1.6
- weight_conv: bfloat16 [640, 5, 640], replicated, may hold values from -0.109375 to 0.109375
- gain_out: float32 [640], replicated, may hold values from 0.4 to 1.6
- weight_out: bfloat16 [1280, 640], replicated, may hold values from -0.25 to 0.25
Outputs:
- grad_input: bfloat16 [12288, 1280], P(('dp', 'shard'))
- grad_weight_in: float32 [1280, 640], P('dp', 'shard')
- grad_weight_conv: float32 [640, 5, 640], P('dp', None, 'shard')
- grad_weight_out: float32 [1280, 640], P('dp', 'shard')
The draws below stay inside these ranges and needn't reach their ends.
Inputs may be any that keep to these rules, and one draw needn't show every extreme that they name: 8 marks an empty slot. All slots of a sequence share one destination. Among the devices of one shard index, every destination receives exactly 384 rows, and one device sends one destination at most one sequence. A device's slots hold whole sequences one after another from its first slot, each in order of position; empty slots come last and hold 0. `length`: 0 on empty slots; equal on all slots of a sequence; every destination receives one sequence of exactly 80 residues. `unmask_order`: within each sequence a permutation of its positions; 0 on empty slots. `timestep`: equal on all slots of a sequence, from 1 to its length; 0 on empty slots.
All inputs are finite; a program needn't handle non-finite values.
Results may differ from the reference program's by a relative error of at most 0.0074.
Values may be sent and summed in bfloat16 or wider, within the bound.
A program may use at most 192 MiB of HBM per device.

```python
import jax
import jax.numpy as jnp
from jax import lax

D = 1280
H = 640
KERNEL_TAPS = 5
DILATION_STEP = 16
LMAX = 80
SEQ_OWN = 6
TOK = 384
LSLOT = 960
OWN_ROWS = 12288
LOAD_ROWS = 30720
N_DP = 8
N_SHARD = 4


def build_layout(key):
    key = jax.random.fold_in(key, 4242)
    key_start, key_size, key_rank, key_time = jax.random.split(key, 4)
    owner_ids = jnp.arange(N_DP, dtype=jnp.int32)
    piece_ids = jnp.arange(SEQ_OWN, dtype=jnp.int32)
    spread = jax.random.randint(key_size, (N_SHARD, N_DP, SEQ_OWN // 2), 0, 17, dtype=jnp.int32)
    spread = spread.at[:, :, 0].set(16)
    piece_sizes = jnp.stack([LMAX - 16 + spread, LMAX - 16 - spread], axis=-1).reshape(N_SHARD, N_DP, SEQ_OWN)
    hot_first = jax.random.randint(key_start, (N_SHARD, 1, 1), 0, N_DP, dtype=jnp.int32)
    crowded = (owner_ids < SEQ_OWN)[None, :, None]
    source = jnp.where(crowded, (hot_first + piece_ids[None, None, :]) % N_DP, (owner_ids[None, :, None] + piece_ids[None, None, :]) % N_DP)
    piece_hits = source[:, None, :, :] == owner_ids[None, :, None, None]
    piece_len = jnp.sum(jnp.where(piece_hits, piece_sizes[:, None, :, :], 0), axis=-1).astype(jnp.int32)
    piece_ends = jnp.cumsum(piece_len, axis=-1).astype(jnp.int32)
    segment_starts = piece_ends - piece_len
    row_ids = jnp.arange(LSLOT, dtype=jnp.int32)
    target = jnp.sum((piece_ends[:, :, None, :] <= row_ids[None, None, :, None]).astype(jnp.int32), axis=-1)
    row_alive = target < N_DP
    owner_safe = jnp.minimum(target, N_DP - 1)
    row_start = jnp.take_along_axis(segment_starts, owner_safe, axis=-1)
    row_len = jnp.where(row_alive, jnp.take_along_axis(piece_len, owner_safe, axis=-1), 0)
    row_position = jnp.where(row_alive, row_ids[None, None, :] - row_start, 0)
    time_bits = jax.random.randint(key_time, (N_SHARD, N_DP, N_DP), 0, 1 << 20, dtype=jnp.int32)
    seq_time = 1 + time_bits % jnp.maximum(piece_len, 1)
    row_time = jnp.where(row_alive, jnp.take_along_axis(seq_time, owner_safe, axis=-1), 0)
    rank_keys = jax.random.randint(key_rank, (N_SHARD, N_DP, LSLOT), 0, 1 << 20, dtype=jnp.int32)
    composite = target * (1 << 20) + rank_keys
    sorted_ids = jnp.argsort(composite, axis=-1, stable=True)
    row_rank = jnp.argsort(sorted_ids, axis=-1, stable=True).astype(jnp.int32)
    row_order = jnp.where(row_alive, row_rank - row_start, 0)
    return (target, row_position, row_len, row_order, row_time)


def flatten_layout(values):
    return jnp.transpose(values, (1, 0, 2)).reshape(-1).astype(jnp.int32)


def draw_destination(key, part):
    return flatten_layout(build_layout(key)[0])


def draw_position(key, part):
    return flatten_layout(build_layout(key)[1])


def draw_length(key, part):
    return flatten_layout(build_layout(key)[2])


def draw_unmask_order(key, part):
    return flatten_layout(build_layout(key)[3])


def draw_timestep(key, part):
    return flatten_layout(build_layout(key)[4])


def strengthened(array, own_key, source, target, shards_of, factor):
    def block_of(dim):
        return (jnp.arange(array.shape[dim]) // (array.shape[dim] // shards_of)).reshape((-1,) + (1,) * (array.ndim - 1 - dim))

    first = jax.random.permutation(own_key, shards_of)[block_of(target)]
    other_side = (block_of(target) + shards_of // 2) % shards_of
    return jnp.where((block_of(source) == first) | (block_of(source) == other_side), factor * array, array)


def shard_levels(stream_key, shape, shards, low, largest):
    def one(axis_at, parts):
        draws = jax.random.uniform(jax.random.fold_in(jax.random.fold_in(stream_key, 6), axis_at), (parts,), jnp.float32, low / len(shards), largest / len(shards))
        return jnp.repeat(jnp.exp(draws), shape[axis_at] // parts).reshape((-1,) + (1,) * (len(shape) - axis_at - 1))

    loudness = one(*shards[0])
    for cut in shards[1:]:
        loudness = loudness * one(*cut)
    return loudness


def noise(own_key, dims, scale, limit, cuts=(), kind=jnp.bfloat16):
    drawn = jax.random.normal(own_key, dims, jnp.float32) * scale
    if len(cuts) > 0:
        drawn = shard_levels(own_key, dims, cuts, -0.22, 0.18) * drawn
    return jnp.clip(drawn, min=-limit, max=limit).astype(kind)


def noise_with(key, extent, scale, most, shards, heavy, kind=jnp.bfloat16):
    drawn = scale * jax.random.normal(key, extent, jnp.float32)
    if shards:
        drawn = drawn * shard_levels(key, extent, shards, -0.22, 0.18)
    return jnp.clip(strengthened(drawn, jax.random.fold_in(key, 3), *heavy), -most, most).astype(kind)


def setup_inputs(seed: int = 0) -> dict:
    keys = jax.random.split(jax.random.key(seed), 15)
    return {
        "embedded": noise(keys[0], (LOAD_ROWS, D), 1.0, 6.0, ((0, 32),)),
        "mask_token_embedding": noise(keys[1], (D,), 1.0, 5.0),
        "destination": draw_destination(jax.random.fold_in(keys[14], 71), 0),
        "position": draw_position(jax.random.fold_in(keys[14], 71), 0),
        "length": draw_length(jax.random.fold_in(keys[14], 71), 0),
        "unmask_order": draw_unmask_order(jax.random.fold_in(keys[14], 71), 0),
        "timestep": draw_timestep(jax.random.fold_in(keys[14], 71), 0),
        "upstream": noise_with(keys[7], (OWN_ROWS, D), 0.05, 0.29882812, ((0, 32),), (0, 1, 32, 2.75)),
        "gain_in": jnp.clip(1.0 + 0.12 * jax.random.normal(keys[8], (D,), jnp.float32), 0.4, 1.6),
        "weight_in": noise(keys[9], (D, H), D ** -0.5, 0.15625),
        "gain_mid": jnp.clip(1.0 + 0.12 * jax.random.normal(keys[10], (H,), jnp.float32), 0.4, 1.6),
        "weight_conv": noise(keys[11], (H, KERNEL_TAPS, H), (KERNEL_TAPS * H) ** -0.5, 0.109375),
        "gain_out": jnp.clip(1.0 + 0.12 * jax.random.normal(keys[12], (H,), jnp.float32), 0.4, 1.6),
        "weight_out": noise(keys[13], (D, H), H ** -0.5, 0.25),
    }


EPS = 1e-05

def normalized_activation(values, gain_vec):
    row_mean = lax.optimization_barrier(jnp.mean(values, axis=-1, keepdims=True))
    centred = values - row_mean
    row_var = lax.optimization_barrier(jnp.mean(centred * centred, axis=-1, keepdims=True))
    return jax.nn.gelu(centred * lax.rsqrt(row_var + EPS) * gain_vec, approximate=False)

def raw_shift(values, offset):
    if offset > 0:
        filler = jnp.zeros((offset, values.shape[1]), values.dtype)
        return jnp.concatenate([values[offset:], filler], axis=0)
    if offset < 0:
        filler = jnp.zeros((-offset, values.shape[1]), values.dtype)
        return jnp.concatenate([filler, values[:offset]], axis=0)
    return values

def contract_rows(left, right):
    return lax.dot_general(left, right, (((0,), (0,)), ((), ())), preferred_element_type=jnp.float32)

def contract_cols(left, right):
    return lax.dot_general(left, right, (((1,), (1,)), ((), ())), preferred_element_type=jnp.float32)

def layer_grads(owner_input, upstream, owner_position, owner_length, gain_in, weight_in, gain_mid, weight_conv, gain_out, weight_out):
    widened_input = owner_input.astype(jnp.float32)
    first_f32, pull_in = jax.vjp(lambda value: normalized_activation(value, gain_in), widened_input)
    first_act = first_f32.astype(jnp.bfloat16)
    hidden = jnp.dot(first_act, weight_in, preferred_element_type=jnp.float32)
    mid_f32, pull_mid = jax.vjp(lambda value: normalized_activation(value, gain_mid), hidden)
    mid_act = mid_f32.astype(jnp.bfloat16)
    tap_offsets = [(kernel_tap_index - KERNEL_TAPS // 2) * DILATION_STEP for kernel_tap_index in range(KERNEL_TAPS)]
    tap_valid = [(owner_position + offset >= 0) & (owner_position + offset < owner_length) for offset in tap_offsets]
    tap_list = [jnp.where(tap_valid[kernel_tap_index][:, None], raw_shift(mid_act, tap_offsets[kernel_tap_index]), jnp.zeros_like(mid_act)) for kernel_tap_index in range(KERNEL_TAPS)]
    conv = jnp.dot(tap_list[0], weight_conv[:, 0, :], preferred_element_type=jnp.float32)
    for kernel_tap_index in range(1, KERNEL_TAPS):
        conv = conv + jnp.dot(tap_list[kernel_tap_index], weight_conv[:, kernel_tap_index, :], preferred_element_type=jnp.float32)
    out_f32, pull_out = jax.vjp(lambda value: normalized_activation(value, gain_out), conv)
    out_act = out_f32.astype(jnp.bfloat16)
    grad_out = contract_rows(upstream, out_act)
    out_cot = jnp.dot(upstream, weight_out, preferred_element_type=jnp.float32)
    conv_cot = pull_out(out_cot)[0].astype(jnp.bfloat16)
    grad_conv = jnp.stack([contract_rows(tap_list[kernel_tap_index], conv_cot) for kernel_tap_index in range(KERNEL_TAPS)], axis=1)
    mid_cot = jnp.zeros(mid_act.shape, jnp.float32)
    for kernel_tap_index in range(KERNEL_TAPS):
        back_term = contract_cols(conv_cot, weight_conv[:, kernel_tap_index, :])
        back_term = jnp.where(tap_valid[kernel_tap_index][:, None], back_term, jnp.zeros_like(back_term))
        mid_cot = mid_cot + raw_shift(back_term, -tap_offsets[kernel_tap_index])
    hidden_cot = pull_mid(mid_cot)[0].astype(jnp.bfloat16)
    grad_in = contract_rows(first_act, hidden_cot)
    input_cot = contract_cols(hidden_cot, weight_in)
    grad_input = (upstream.astype(jnp.float32) + pull_in(input_cot)[0]).astype(jnp.bfloat16)
    return (grad_input, grad_in, grad_conv, grad_out)

def reference(embedded, mask_token_embedding, destination, position, length, unmask_order, timestep, upstream, gain_in, weight_in, gain_mid, weight_conv, gain_out, weight_out):
    channels = embedded.shape[1]
    masked_input = jnp.where((unmask_order < timestep)[:, None], mask_token_embedding[None, :], embedded)

    def regroup(values, slots):
        tail = values.shape[1:]
        grouped = values.reshape((N_DP, N_SHARD, slots) + tail)
        return jnp.moveaxis(grouped, 1, 0).reshape((N_SHARD, N_DP * slots) + tail)

    def one_group(pieces):
        group_rows, group_dest, group_pos, group_len, group_up = pieces
        ordering = jnp.argsort(group_dest, stable=True)[:N_DP * TOK].astype(jnp.int32)
        return layer_grads(group_rows[ordering], group_up, group_pos[ordering], group_len[ordering], gain_in, weight_in, gain_mid, weight_conv, gain_out, weight_out)
    grouped_inputs = (regroup(masked_input, LSLOT), regroup(destination, LSLOT), regroup(position, LSLOT), regroup(length, LSLOT), regroup(upstream, TOK))
    grad_rows, grad_in, grad_conv, grad_out = lax.map(one_group, grouped_inputs)
    grad_input = jnp.moveaxis(grad_rows.reshape(N_SHARD, N_DP, TOK, channels), 0, 1).reshape(N_DP * N_SHARD * TOK, channels)
    return (grad_input, lax.optimization_barrier(jnp.sum(grad_in, axis=0)), lax.optimization_barrier(jnp.sum(grad_conv, axis=0)), lax.optimization_barrier(jnp.sum(grad_out, axis=0)))
```

```python
import jax
import jax.numpy as jnp
from jax import lax
from jax.experimental import pallas as pl
from jax.experimental.pallas import tpu as pltpu
import functools
from jax.sharding import PartitionSpec as P

KERNEL_TAPS = 5
DILATION_STEP = 16
LMAX = 80


EPS = 1e-05


def raw_shift(values, offset):
    if offset > 0:
        filler = jnp.zeros((offset, values.shape[1]), values.dtype)
        return jnp.concatenate([values[offset:], filler], axis=0)
    if offset < 0:
        filler = jnp.zeros((-offset, values.shape[1]), values.dtype)
        return jnp.concatenate([filler, values[:offset]], axis=0)
    return values


def contract_rows(left, right):
    return lax.dot_general(
        left, right, (((0,), (0,)), ((), ())), preferred_element_type=jnp.float32
    )


def contract_cols(left, right):
    return lax.dot_general(
        left, right, (((1,), (1,)), ((), ())), preferred_element_type=jnp.float32
    )


MESH = pl.DeviceIdType.MESH


def bit_orders(owners, groups):
    dp_bits = [("dp", i) for i in range(owners.bit_length() - 1)]
    sh_bits = [("shard", i) for i in range(groups.bit_length() - 1)]
    first, others = sh_bits[:1], sh_bits[1:]
    return (
        first + others + dp_bits,
        first + dp_bits[:1] + others + dp_bits[1:],
        first + dp_bits[1:] + others + dp_bits[:1],
    )


def chunk_rows(rows):
    unit = rows // 5
    return (2 * unit, 2 * unit, unit)


def round_up(value, multiple):
    return -(-value // multiple) * multiple


def placed(values, offset):
    low = offset // 128 * 128
    high = round_up(offset + values.shape[1], 128)
    parts = []
    if offset > low:
        parts.append(jnp.zeros((values.shape[0], offset - low), values.dtype))
    parts.append(values)
    if high > offset + values.shape[1]:
        parts.append(jnp.zeros((values.shape[0], high - offset - values.shape[1]), values.dtype))
    return low, (jnp.concatenate(parts, axis=1) if len(parts) > 1 else values)


FILL = 64.0
INV_SQRT2 = 0.7071067811865476
INV_SQRT_2PI = 0.3989422804014327
VMEM_LIMIT = 60 * 1024 * 1024


def flipped(index, mask):
    other, bit = index, 0
    while (mask >> bit) > 0:
        if (mask >> bit) & 1:
            other = other + (1 - 2 * lax.rem(index // (1 << bit), 2)) * (1 << bit)
        bit += 1
    return other


def dispatch_kernel(
    owners,
    destination,
    position,
    order,
    timestep,
    token,
    embedded,
    bucket,
    bucket_pos,
    bucket_len,
    sent,
    got,
    send_sem,
    recv_sem,
):
    me, group = lax.axis_index("dp"), lax.axis_index("shard")
    barrier = pltpu.get_barrier_semaphore()
    for j in range(1, owners):
        pl.semaphore_signal(
            barrier, inc=1, device_id=(flipped(me, j), group), device_id_type=MESH
        )
    slot = jnp.where(destination[...] < owners, destination[...] * LMAX + position[...], -1)
    hidden_slot = (order[...] < timestep[...]).astype(jnp.float32)

    def block_for(owner):
        rows = lax.broadcasted_iota(jnp.int32, (LMAX, slot.shape[1]), 0) + owner * LMAX
        pick = (rows == slot).astype(jnp.float32)
        live = jnp.sum(pick, axis=1, keepdims=True)
        masked = jnp.sum(pick * hidden_slot, axis=1, keepdims=True)
        block = jnp.dot(
            pick.astype(jnp.bfloat16), embedded[...], preferred_element_type=jnp.float32
        )
        block = jnp.where(masked > 0.5, token[...].astype(jnp.float32), block)
        return jnp.where(live > 0.5, block, FILL).astype(jnp.bfloat16)

    copies = []
    for j in range(owners - 1, 0, -1):
        other = flipped(me, j)
        sent[j] = block_for(other)
        if j == owners - 1:
            pl.semaphore_wait(barrier, owners - 1)
        copy = pltpu.make_async_remote_copy(
            src_ref=sent.at[j],
            dst_ref=got.at[me],
            send_sem=send_sem.at[j],
            recv_sem=recv_sem.at[j],
            device_id=(other, group),
            device_id_type=MESH,
        )
        copy.start()
        copies.append(copy)
    got[me] = block_for(me)
    for copy in copies:
        copy.wait_recv()
    lanes = lax.broadcasted_iota(jnp.int32, (1, owners * LMAX), 1)
    place_of = jnp.full((1, owners * LMAX), -1, jnp.int32)
    pos_of = jnp.zeros((1, owners * LMAX), jnp.float32)
    len_of = jnp.zeros((1, owners * LMAX), jnp.float32)
    start = jnp.zeros((1, 1), jnp.int32)
    for source in range(owners):
        marks = got[source, :, 0:128].astype(jnp.float32)[:, 0:1]
        count = jnp.sum((marks < FILL / 2).astype(jnp.float32), axis=0, keepdims=True)
        whole = count.astype(jnp.int32)
        inside = lanes - source * LMAX
        used = (inside >= 0) & (inside < whole)
        place_of = jnp.where(used, start + inside, place_of)
        pos_of = jnp.where(used, inside.astype(jnp.float32), pos_of)
        len_of = jnp.where(used, count, len_of)
        start = start + whole
    own = bucket.shape[0]
    take = (
        lax.broadcasted_iota(jnp.int32, (own, owners * LMAX), 0) == place_of
    ).astype(jnp.float32)
    bucket_pos[...] = jnp.sum(take * pos_of, axis=1, keepdims=True).astype(jnp.int32)
    bucket_len[...] = jnp.sum(take * len_of, axis=1, keepdims=True).astype(jnp.int32)
    bucket[...] = jnp.dot(
        take.astype(jnp.bfloat16),
        got[...].reshape(owners * LMAX, bucket.shape[1]),
        preferred_element_type=jnp.float32,
    ).astype(jnp.bfloat16)
    for copy in copies:
        copy.wait_send()


def looped(rows, step, body):
    def run(i, carry):
        body(pl.ds(pl.multiple_of(i * step, step), step))
        return carry

    lax.fori_loop(0, rows // step, run, 0)


def normalize(value):
    centred = value - jnp.mean(value, axis=-1, keepdims=True)
    scale = lax.rsqrt(jnp.mean(centred * centred, axis=-1, keepdims=True) + EPS)
    return centred * scale, scale


def gelu_parts(scaled):
    half = 0.5 * (1.0 + lax.erf(scaled * INV_SQRT2))
    slope = half + scaled * (INV_SQRT_2PI * jnp.exp(-0.5 * scaled * scaled))
    return scaled * half, slope


def pull_back(cot, normal, scale):
    inner = jnp.mean(cot * normal, axis=-1, keepdims=True)
    return scale * (cot - jnp.mean(cot, axis=-1, keepdims=True) - normal * inner)


def part_layouts(narrow, wide):
    early = KERNEL_TAPS - 1
    return (
        ((0, early * narrow), (early * narrow, wide)),
        ((0, narrow), (narrow, wide)),
    )


def span_of(offset, size):
    return round_up(offset + size, 128) - offset // 128 * 128


def width_of(layout):
    return round_up(layout[-1][0] + layout[-1][1], 128)


def layer_kernel(
    owners,
    groups,
    position,
    length,
    owner_input,
    upstream,
    gain_in,
    gain_mid,
    gain_out,
    weight_in_hbm,
    weight_conv_hbm,
    weight_out_hbm,
    grad_input,
    grad_in,
    grad_conv,
    grad_out,
    *scratch,
):
    chunks = 3
    terms = (scratch[0:3], scratch[3:6])
    got = (scratch[6:9], scratch[9:12])
    left_conv, left_out, left_last, left_in = scratch[12:16]
    right_conv, right_out, right_in = scratch[16:19]
    weight_in, weight_conv, weight_out = scratch[19:22]
    first, mid, out_act, conv_cot, hidden_cot, taps = scratch[22:28]
    hidden, mid_gain, mid_scale, wide_a, wide_b = scratch[28:33]
    send_sem, recv_sem, load_sem = scratch[33:36]

    orders = bit_orders(owners, groups)
    steps = len(orders[0])
    total = 1 << steps
    me = {"dp": lax.axis_index("dp"), "shard": lax.axis_index("shard")}
    own_rows = owner_input.shape[0]
    narrow, wide = mid.shape[1] // owners, first.shape[1] // owners
    rows = right_conv.shape[0] // groups
    layouts = part_layouts(narrow, wide)

    def bit_of(axis, bit):
        return lax.rem(me[axis] // (1 << bit), 2)

    def partner(axis, bit):
        other = me[axis] + (1 - 2 * bit_of(axis, bit)) * (1 << bit)
        return (other, me["shard"]) if axis == "dp" else (me["dp"], other)

    loads = [
        pltpu.make_async_copy(source, target, load_sem.at[i])
        for i, (source, target) in enumerate(
            (
                (weight_out_hbm, weight_out),
                (weight_in_hbm, weight_in),
                (weight_conv_hbm, weight_conv),
            )
        )
    ]
    for load in loads:
        load.start()
    barrier = pltpu.get_barrier_semaphore()
    for axis, bit in orders[0]:
        pl.semaphore_signal(barrier, inc=1, device_id=partner(axis, bit), device_id_type=MESH)

    tap_offsets = [(k - KERNEL_TAPS // 2) * DILATION_STEP for k in range(KERNEL_TAPS)]

    def fill_taps(source, sign):
        for k, base_offset in enumerate(tap_offsets):
            offset = sign * base_offset
            moved = position[...] + offset
            valid = (moved >= 0) & (moved < length[...])
            shifted = raw_shift(source[...], offset)
            taps[k] = jnp.where(valid, shifted.astype(jnp.float32), 0.0).astype(jnp.bfloat16)

    def place(left, pieces, offset):
        for owner in range(owners):
            values = pieces(owner)
            left[owner] = placed(values, offset)[1].astype(jnp.bfloat16)

    def wide_piece(source):
        return lambda owner: source[:, owner * wide : (owner + 1) * wide].astype(jnp.float32)

    def half_terms(part, low_bit, sides):
        starts = [(2 * i + low_bit) * rows for i in range(groups // 2)]
        outs = terms[part]
        width = outs[0].shape[2]

        def body(owner, carry):
            tiles = [None] * (width // 128)
            for left, right, offset in sides:
                low = offset // 128
                picked = [right[pl.ds(pl.multiple_of(s, 16), rows), :] for s in starts]
                picked = picked[0] if len(picked) == 1 else jnp.concatenate(picked, axis=0)
                term = jnp.dot(picked, left[owner], preferred_element_type=jnp.float32)
                for j in range(left.shape[2] // 128):
                    piece = term[:, j * 128 : (j + 1) * 128]
                    held = tiles[low + j]
                    tiles[low + j] = piece if held is None else held + piece
            for j, tile in enumerate(tiles):
                tile = tile.astype(jnp.bfloat16)
                for i in range(groups // 2):
                    at = i * rows
                    for order, out in zip(orders, outs):
                        index = low_bit
                        for axis, bit in order[1:]:
                            if axis == "dp":
                                index = index * 2 + lax.rem(owner // (1 << bit), 2)
                            else:
                                index = index * 2 + (((2 * i) >> bit) & 1)
                        count = out.shape[1]
                        out[index, :, j * 128 : (j + 1) * 128] = tile[at : at + count]
                        at += count
            return carry

        lax.fori_loop(0, owners, body, 0)

    base, at = [], 0
    for t in range(steps):
        base.append(at)
        at += total >> (t + 1)

    def copy_of(part, c, t):
        half = total >> (t + 1)
        away = 1 - bit_of(*orders[c][t])
        source = terms[part][c] if t == 0 else got[part][c]
        start = away * half if t == 0 else base[t - 1] + away * half
        return pltpu.make_async_remote_copy(
            src_ref=source.at[pl.ds(start, half)],
            dst_ref=got[part][c].at[pl.ds(base[t], half)],
            send_sem=send_sem.at[part, c, t],
            recv_sem=recv_sem.at[part, c, t],
            device_id=partner(*orders[c][t]),
            device_id_type=MESH,
        )

    copies = [
        [[copy_of(part, c, t) for t in range(steps)] for c in range(chunks)] for part in range(2)
    ]

    def summed(part, c, t, at):
        half = total >> (t + 1)
        kept = bit_of(*orders[c][t]) * half
        source = terms[part][c] if t == 0 else got[part][c]
        offset = kept if t == 0 else base[t - 1] + kept
        here = got[part][c]
        return source[offset + at].astype(jnp.float32) + here[base[t] + at].astype(jnp.float32)

    def add(part, c, t, first_block, count):
        def body(i, carry):
            at = first_block + i
            got[part][c][base[t] + at] = summed(part, c, t, at).astype(jnp.bfloat16)
            return carry

        lax.fori_loop(0, count, body, 0)

    def advance(part, t):
        half = total >> (t + 2)
        for c in range(chunks):
            copies[part][c][t].wait_recv()
            nxt = bit_of(*orders[c][t + 1])
            add(part, c, t, (1 - nxt) * half, half)
            copies[part][c][t + 1].start()
        for c in range(chunks):
            nxt = bit_of(*orders[c][t + 1])
            add(part, c, t, nxt * half, half)

    def finish(part):
        finished = []
        for c in range(chunks):
            copies[part][c][steps - 1].wait_recv()
            finished.append(summed(part, c, steps - 1, 0))
        return jnp.concatenate(finished, axis=0).T

    place(left_out, wide_piece(upstream), layouts[0][1][0])
    loads[0].wait()
    wide_a[...] = jnp.dot(upstream[...], weight_out[...], preferred_element_type=jnp.float32)

    def first_rows(at):
        normal, _ = normalize(owner_input[at, :].astype(jnp.float32))
        first[at, :] = gelu_parts(normal * gain_in[...])[0].astype(jnp.bfloat16)

    looped(own_rows, 32, first_rows)
    loads[1].wait()
    hidden[...] = jnp.dot(first[...], weight_in[...], preferred_element_type=jnp.float32)

    def mid_rows(at):
        normal, scale = normalize(hidden[at, :])
        act, slope = gelu_parts(normal * gain_mid[...])
        mid[at, :] = act.astype(jnp.bfloat16)
        hidden[at, :] = normal
        mid_gain[at, :] = slope * gain_mid[...]
        mid_scale[at, :] = scale

    looped(own_rows, 32, mid_rows)
    fill_taps(mid, 1)
    loads[2].wait()
    conv = jnp.dot(taps[0], weight_conv[0], preferred_element_type=jnp.float32)
    for k in range(1, KERNEL_TAPS):
        conv = conv + jnp.dot(taps[k], weight_conv[k], preferred_element_type=jnp.float32)
    wide_b[...] = conv

    def out_rows(at):
        normal, scale = normalize(wide_b[at, :])
        act, slope = gelu_parts(normal * gain_out[...])
        out_act[at, :] = act.astype(jnp.bfloat16)
        cot = wide_a[at, :] * slope * gain_out[...]
        conv_cot[at, :] = pull_back(cot, normal, scale).astype(jnp.bfloat16)

    looped(own_rows, 32, out_rows)

    def tap_piece(ks):
        def piece(owner):
            here = slice(owner * narrow, (owner + 1) * narrow)
            parts = [taps[k, :, here].astype(jnp.float32) for k in ks]
            return parts[0] if len(parts) == 1 else jnp.concatenate(parts, axis=1)

        return piece

    place(left_conv, tap_piece(range(KERNEL_TAPS - 1)), layouts[0][0][0])
    right_conv[...] = conv_cot[...].T
    right_out[...] = out_act[...].T
    mine = bit_of(*orders[0][0])
    sides = (
        (
            (left_conv, right_conv, layouts[0][0][0]),
            (left_out, right_out, layouts[0][1][0]),
        ),
        (
            (left_last, right_conv, layouts[1][0][0]),
            (left_in, right_in, layouts[1][1][0]),
        ),
    )
    half_terms(0, 1 - mine, sides[0])
    pl.semaphore_wait(barrier, steps)
    for c in range(chunks):
        copies[0][c][0].start()
    half_terms(0, mine, sides[0])
    place(left_last, tap_piece((KERNEL_TAPS - 1,)), layouts[1][0][0])
    place(left_in, wide_piece(first), layouts[1][1][0])
    fill_taps(conv_cot, -1)
    advance(0, 0)
    mid_cot = contract_cols(taps[0], weight_conv[0])
    for k in range(1, KERNEL_TAPS):
        mid_cot = mid_cot + contract_cols(taps[k], weight_conv[k])
    wide_b[...] = mid_cot

    def hidden_rows(at):
        cot = wide_b[at, :] * mid_gain[at, :]
        hidden_cot[at, :] = pull_back(cot, hidden[at, :], mid_scale[at, :]).astype(jnp.bfloat16)

    looped(own_rows, 32, hidden_rows)
    right_in[...] = hidden_cot[...].T
    half_terms(1, 1 - mine, sides[1])
    for c in range(chunks):
        copies[1][c][0].start()
    half_terms(1, mine, sides[1])
    advance(0, 1)
    advance(1, 0)

    def input_rows(start):
        piece = jnp.concatenate([wide_a[start, :], wide_b[start, :]], axis=1)
        normal, scale = normalize(owner_input[start, :].astype(jnp.float32))
        slope = gelu_parts(normal * gain_in[...])[1]
        grad = pull_back(piece * slope * gain_in[...], normal, scale)
        grad_input[start, :] = (upstream[start, :].astype(jnp.float32) + grad).astype(
            jnp.bfloat16
        )

    halves = weight_in.shape[0] // 2
    wide_a[...] = contract_cols(hidden_cot[...], weight_in[:halves])
    wide_b[...] = contract_cols(hidden_cot[...], weight_in[halves:])
    looped(own_rows // 2, 32, input_rows)
    advance(0, 2)
    advance(1, 1)
    looped_from = own_rows // 2

    def late_rows(at):
        input_rows(pl.ds(pl.multiple_of(at.start + looped_from, 32), 32))

    looped(own_rows // 2, 32, late_rows)
    for t in range(3, steps):
        advance(0, t) if t < steps - 1 else None
        advance(1, t - 1)
    early = finish(0)
    for k in range(KERNEL_TAPS - 1):
        grad_conv[k] = early[k * narrow : (k + 1) * narrow]
    at = layouts[0][1][0]
    grad_out[...] = early[at : at + wide]
    late = finish(1)
    grad_conv[KERNEL_TAPS - 1] = late[:narrow]
    grad_in[...] = late[narrow : narrow + wide]
    for part in range(2):
        for c in range(chunks):
            for t in range(steps):
                copies[part][c][t].wait_send()


def local(
    embedded,
    mask_token_embedding,
    destination,
    position,
    length,
    unmask_order,
    timestep,
    upstream,
    gain_in,
    weight_in,
    gain_mid,
    weight_conv,
    gain_out,
    weight_out,
):
    channels = embedded.shape[1]
    owners, groups = lax.axis_size("dp"), lax.axis_size("shard")
    own_rows = upstream.shape[0]
    inner = weight_in.shape[1]
    vmem = pl.BlockSpec(memory_space=pltpu.VMEM)
    bucket, bucket_pos, bucket_len = pl.pallas_call(
        functools.partial(dispatch_kernel, owners),
        out_shape=[
            jax.ShapeDtypeStruct((own_rows, channels), jnp.bfloat16),
            jax.ShapeDtypeStruct((own_rows, 1), jnp.int32),
            jax.ShapeDtypeStruct((own_rows, 1), jnp.int32),
        ],
        in_specs=[vmem] * 6,
        out_specs=[vmem] * 3,
        scratch_shapes=[
            pltpu.VMEM((owners, LMAX, channels), jnp.bfloat16),
            pltpu.VMEM((owners, LMAX, channels), jnp.bfloat16),
            pltpu.SemaphoreType.DMA((owners,)),
            pltpu.SemaphoreType.DMA((owners,)),
        ],
        compiler_params=pltpu.CompilerParams(
            collective_id=1, has_side_effects=True, vmem_limit_bytes=VMEM_LIMIT
        ),
        name="dispatch",
    )(
        destination[None, :],
        position[None, :],
        unmask_order[None, :],
        timestep[None, :],
        mask_token_embedding[None, :],
        embedded,
    )
    narrow, wide, rows = inner // owners, channels // owners, inner // groups
    layouts = part_layouts(narrow, wide)
    total = owners * groups
    steps = total.bit_length() - 1
    counts = chunk_rows(rows)
    hbm = pl.BlockSpec(memory_space=pl.ANY)
    grad_input, grad_in, grad_conv, grad_out = pl.pallas_call(
        functools.partial(layer_kernel, owners, groups),
        out_shape=[
            jax.ShapeDtypeStruct((own_rows, channels), jnp.bfloat16),
            jax.ShapeDtypeStruct((wide, rows), jnp.float32),
            jax.ShapeDtypeStruct((KERNEL_TAPS, narrow, rows), jnp.float32),
            jax.ShapeDtypeStruct((wide, rows), jnp.float32),
        ],
        in_specs=[vmem] * 7 + [hbm] * 3,
        out_specs=[vmem] * 4,
        scratch_shapes=[
            pltpu.VMEM((total, n, width_of(layout)), jnp.bfloat16)
            for layout in layouts
            for n in counts
        ]
        + [
            pltpu.VMEM((total - 1, n, width_of(layout)), jnp.bfloat16)
            for layout in layouts
            for n in counts
        ]
        + [
            pltpu.VMEM((owners, own_rows, span_of(*item)), jnp.bfloat16)
            for layout in layouts
            for item in layout
        ]
        + [pltpu.VMEM((inner, own_rows), jnp.bfloat16)] * 3
        + [
            pltpu.VMEM((channels, inner), jnp.bfloat16),
            pltpu.VMEM((KERNEL_TAPS, inner, inner), jnp.bfloat16),
            pltpu.VMEM((channels, inner), jnp.bfloat16),
            pltpu.VMEM((own_rows, channels), jnp.bfloat16),
        ]
        + [pltpu.VMEM((own_rows, inner), jnp.bfloat16)] * 4
        + [pltpu.VMEM((KERNEL_TAPS, own_rows, inner), jnp.bfloat16)]
        + [
            pltpu.VMEM((own_rows, inner), jnp.float32),
            pltpu.VMEM((own_rows, inner), jnp.float32),
            pltpu.VMEM((own_rows, 1), jnp.float32),
            pltpu.VMEM((own_rows, inner), jnp.float32),
            pltpu.VMEM((own_rows, inner), jnp.float32),
        ]
        + [
            pltpu.SemaphoreType.DMA((2, 3, steps)),
            pltpu.SemaphoreType.DMA((2, 3, steps)),
            pltpu.SemaphoreType.DMA((3,)),
        ],
        compiler_params=pltpu.CompilerParams(
            collective_id=0, has_side_effects=True, vmem_limit_bytes=VMEM_LIMIT
        ),
        name="layer",
    )(
        bucket_pos,
        bucket_len,
        bucket,
        upstream,
        gain_in[None, :],
        gain_mid[None, :],
        gain_out[None, :],
        weight_in,
        jnp.transpose(weight_conv, (1, 0, 2)),
        weight_out,
    )
    return grad_input, grad_in, jnp.transpose(grad_conv, (1, 0, 2)), grad_out


def solution(mesh):
    return jax.shard_map(
        local,
        mesh=mesh,
        in_specs=(
            P(("dp", "shard"), None),
            P(),
            P(("dp", "shard")),
            P(("dp", "shard")),
            P(("dp", "shard")),
            P(("dp", "shard")),
            P(("dp", "shard")),
            P(("dp", "shard"), None),
            P(),
            P(),
            P(),
            P(),
            P(),
            P(),
        ),
        out_specs=(
            P(("dp", "shard"), None),
            P("dp", "shard"),
            P("dp", None, "shard"),
            P("dp", "shard"),
        ),
        check_vma=False,
    )
```

```python
import jax
import jax.numpy as jnp
from jax import lax
from jax.experimental import pallas as pl
from jax.experimental.pallas import tpu as pltpu
import functools
from jax.sharding import PartitionSpec as P

KERNEL_TAPS = 5
DILATION_STEP = 16
LMAX = 80


EPS = 1e-05


def raw_shift(values, offset):
    if offset > 0:
        filler = jnp.zeros((offset, values.shape[1]), values.dtype)
        return jnp.concatenate([values[offset:], filler], axis=0)
    if offset < 0:
        filler = jnp.zeros((-offset, values.shape[1]), values.dtype)
        return jnp.concatenate([filler, values[:offset]], axis=0)
    return values


def contract_rows(left, right):
    return lax.dot_general(
        left, right, (((0,), (0,)), ((), ())), preferred_element_type=jnp.float32
    )


def contract_cols(left, right):
    return lax.dot_general(
        left, right, (((1,), (1,)), ((), ())), preferred_element_type=jnp.float32
    )


MESH = pl.DeviceIdType.MESH


def bit_orders(owners, groups):
    dp_bits = [("dp", i) for i in range(owners.bit_length() - 1)]
    chip_bits = [("shard", i) for i in range(1, groups.bit_length() - 1)]
    return (
        chip_bits + dp_bits,
        dp_bits[:1] + chip_bits + dp_bits[1:],
        dp_bits[1:] + chip_bits + dp_bits[:1],
    )


def chunk_rows(rows):
    unit = rows // 5
    return (2 * unit, 2 * unit, unit)


def round_up(value, multiple):
    return -(-value // multiple) * multiple


def placed(values, offset):
    low = offset // 128 * 128
    high = round_up(offset + values.shape[1], 128)
    parts = []
    if offset > low:
        parts.append(jnp.zeros((values.shape[0], offset - low), values.dtype))
    parts.append(values)
    if high > offset + values.shape[1]:
        parts.append(jnp.zeros((values.shape[0], high - offset - values.shape[1]), values.dtype))
    return low, (jnp.concatenate(parts, axis=1) if len(parts) > 1 else values)


FILL = 64.0
INV_SQRT2 = 0.7071067811865476
INV_SQRT_2PI = 0.3989422804014327
VMEM_LIMIT = 60 * 1024 * 1024


def flipped(index, mask):
    other, bit = index, 0
    while (mask >> bit) > 0:
        if (mask >> bit) & 1:
            other = other + (1 - 2 * lax.rem(index // (1 << bit), 2)) * (1 << bit)
        bit += 1
    return other


def dispatch_kernel(
    owners,
    destination,
    position,
    order,
    timestep,
    token,
    embedded,
    bucket,
    bucket_pos,
    bucket_len,
    sent,
    got,
    send_sem,
    recv_sem,
):
    me, group = lax.axis_index("dp"), lax.axis_index("shard")
    barrier = pltpu.get_barrier_semaphore()
    for j in range(1, owners):
        pl.semaphore_signal(
            barrier, inc=1, device_id=(flipped(me, j), group), device_id_type=MESH
        )
    slot = jnp.where(destination[...] < owners, destination[...] * LMAX + position[...], -1)
    hidden_slot = (order[...] < timestep[...]).astype(jnp.float32)

    def block_for(owner):
        rows = lax.broadcasted_iota(jnp.int32, (LMAX, slot.shape[1]), 0) + owner * LMAX
        pick = (rows == slot).astype(jnp.float32)
        live = jnp.sum(pick, axis=1, keepdims=True)
        masked = jnp.sum(pick * hidden_slot, axis=1, keepdims=True)
        block = jnp.dot(
            pick.astype(jnp.bfloat16), embedded[...], preferred_element_type=jnp.float32
        )
        block = jnp.where(masked > 0.5, token[...][None, :].astype(jnp.float32), block)
        return jnp.where(live > 0.5, block, FILL).astype(jnp.bfloat16)

    copies = []
    for j in range(owners - 1, 0, -1):
        other = flipped(me, j)
        sent[j] = block_for(other)
        if j == owners - 1:
            pl.semaphore_wait(barrier, owners - 1)
        copy = pltpu.make_async_remote_copy(
            src_ref=sent.at[j],
            dst_ref=got.at[me],
            send_sem=send_sem.at[j],
            recv_sem=recv_sem.at[j],
            device_id=(other, group),
            device_id_type=MESH,
        )
        copy.start()
        copies.append(copy)
    got[me] = block_for(me)
    for copy in copies:
        copy.wait_recv()
    lanes = lax.broadcasted_iota(jnp.int32, (1, owners * LMAX), 1)
    place_of = jnp.full((1, owners * LMAX), -1, jnp.int32)
    pos_of = jnp.zeros((1, owners * LMAX), jnp.float32)
    len_of = jnp.zeros((1, owners * LMAX), jnp.float32)
    start = jnp.zeros((1, 1), jnp.int32)
    for source in range(owners):
        marks = got[source, :, 0:128].astype(jnp.float32)[:, 0:1]
        count = jnp.sum((marks < FILL / 2).astype(jnp.float32), axis=0, keepdims=True)
        whole = count.astype(jnp.int32)
        inside = lanes - source * LMAX
        used = (inside >= 0) & (inside < whole)
        place_of = jnp.where(used, start + inside, place_of)
        pos_of = jnp.where(used, inside.astype(jnp.float32), pos_of)
        len_of = jnp.where(used, count, len_of)
        start = start + whole
    own = bucket.shape[0]
    take = (
        lax.broadcasted_iota(jnp.int32, (own, owners * LMAX), 0) == place_of
    ).astype(jnp.float32)
    bucket_pos[...] = jnp.sum(take * pos_of, axis=1, keepdims=True).astype(jnp.int32)
    bucket_len[...] = jnp.sum(take * len_of, axis=1, keepdims=True).astype(jnp.int32)
    bucket[...] = jnp.dot(
        take.astype(jnp.bfloat16),
        got[...].reshape(owners * LMAX, bucket.shape[1]),
        preferred_element_type=jnp.float32,
    ).astype(jnp.bfloat16)
    for copy in copies:
        copy.wait_send()


def looped(rows, step, body):
    def run(i, carry):
        body(pl.ds(pl.multiple_of(i * step, step), step))
        return carry

    lax.fori_loop(0, rows // step, run, 0)


def normalize(value):
    centred = value - jnp.mean(value, axis=-1, keepdims=True)
    scale = lax.rsqrt(jnp.mean(centred * centred, axis=-1, keepdims=True) + EPS)
    return centred * scale, scale


def gelu_parts(scaled):
    half = 0.5 * (1.0 + lax.erf(scaled * INV_SQRT2))
    slope = half + scaled * (INV_SQRT_2PI * jnp.exp(-0.5 * scaled * scaled))
    return scaled * half, slope


def pull_back(cot, normal, scale):
    inner = jnp.mean(cot * normal, axis=-1, keepdims=True)
    return scale * (cot - jnp.mean(cot, axis=-1, keepdims=True) - normal * inner)


def part_layouts(narrow, wide):
    early = KERNEL_TAPS - 1
    return (
        ((0, early * narrow), (early * narrow, wide)),
        ((0, narrow), (narrow, wide)),
    )


def span_of(offset, size):
    return round_up(offset + size, 128) - offset // 128 * 128


def width_of(layout):
    return round_up(layout[-1][0] + layout[-1][1], 128)


def layer_kernel(
    owners,
    groups,
    position,
    length,
    owner_input,
    upstream,
    gain_in,
    gain_mid,
    gain_out,
    weight_in_hbm,
    weight_conv_hbm,
    weight_out_hbm,
    grad_input,
    early_sum,
    late_sum,
    *scratch,
):
    chunks = 3
    terms = (scratch[0:3], scratch[3:6])
    got = (scratch[6:9], scratch[9:12])
    left_conv, left_out, left_last, left_in = scratch[12:16]
    right_conv, right_out, right_in = scratch[16:19]
    weight_in, weight_conv, weight_out = scratch[19:22]
    first, mid, out_act, conv_cot, hidden_cot, taps = scratch[22:28]
    hidden, mid_gain, mid_scale, wide_a, wide_b = scratch[28:33]
    right_conv_peer, right_out_peer, right_in_peer = scratch[33:36]
    send_sem, recv_sem, load_sem, factor_send, factor_recv = scratch[36:41]

    orders = bit_orders(owners, groups)
    steps = len(orders[0])
    total = 1 << steps
    me = {"dp": lax.axis_index("dp"), "shard": lax.axis_index("shard")}
    own_rows = owner_input.shape[0]
    narrow, wide = mid.shape[1] // owners, first.shape[1] // owners
    rows = right_conv.shape[2]
    layouts = part_layouts(narrow, wide)

    def bit_of(axis, bit):
        return lax.rem(me[axis] // (1 << bit), 2)

    def partner(axis, bit):
        other = me[axis] + (1 - 2 * bit_of(axis, bit)) * (1 << bit)
        return (other, me["shard"]) if axis == "dp" else (me["dp"], other)

    loads = [
        pltpu.make_async_copy(source, target, load_sem.at[i])
        for i, (source, target) in enumerate(
            (
                (weight_out_hbm, weight_out),
                (weight_in_hbm, weight_in),
                (weight_conv_hbm, weight_conv),
            )
        )
    ]
    for load in loads:
        load.start()
    barrier = pltpu.get_barrier_semaphore()
    for axis, bit in [("shard", 0)] + orders[0]:
        pl.semaphore_signal(barrier, inc=1, device_id=partner(axis, bit), device_id_type=MESH)
    core = bit_of("shard", 0)

    def to_other_core(number, source, target):
        return pltpu.make_async_remote_copy(
            src_ref=source,
            dst_ref=target,
            send_sem=factor_send.at[number],
            recv_sem=factor_recv.at[number],
            device_id=partner("shard", 0),
            device_id_type=MESH,
        )

    lefts = (left_conv, left_out, left_last, left_in)
    left_copies = [to_other_core(n, ref.at[0], ref.at[1]) for n, ref in enumerate(lefts)]
    rights = ((right_conv, right_conv_peer), (right_out, right_out_peer), (right_in, right_in_peer))
    right_copies = [
        to_other_core(4 + n, ref.at[1 - core], peer) for n, (ref, peer) in enumerate(rights)
    ]

    def turn(right, values):
        turned = values[...].T
        for g in range(groups):
            right[g % 2, g // 2] = turned[g * rows : (g + 1) * rows]

    tap_offsets = [(k - KERNEL_TAPS // 2) * DILATION_STEP for k in range(KERNEL_TAPS)]

    def fill_taps(source, sign):
        for k, base_offset in enumerate(tap_offsets):
            offset = sign * base_offset
            moved = position[...] + offset
            valid = (moved >= 0) & (moved < length[...])
            shifted = raw_shift(source[...], offset)
            taps[k] = jnp.where(valid, shifted.astype(jnp.float32), 0.0).astype(jnp.bfloat16)

    def place(left, pieces, offset):
        for owner in range(owners):
            values = pieces(owner)
            left[0, owner] = placed(values, offset)[1].astype(jnp.bfloat16)

    def wide_piece(source):
        return lambda owner: source[:, owner * wide : (owner + 1) * wide].astype(jnp.float32)

    def multiply(part, low_bit, sides):
        outs = terms[part]
        width = outs[0].shape[2]

        def body(pair, carry):
            owner = pair * 2 + low_bit
            tiles = [None] * (width // 128)
            for left, (right, peer), offset in sides:
                low = offset // 128
                picked = jnp.concatenate(
                    [
                        right[core].reshape(groups // 2 * rows, own_rows),
                        peer[...].reshape(groups // 2 * rows, own_rows),
                    ],
                    axis=1,
                )
                both = jnp.concatenate([left[0, owner], left[1, owner]], axis=0)
                term = jnp.dot(picked, both, preferred_element_type=jnp.float32)
                for j in range(left.shape[3] // 128):
                    piece = term[:, j * 128 : (j + 1) * 128]
                    held = tiles[low + j]
                    tiles[low + j] = piece if held is None else held + piece
            for j, tile in enumerate(tiles):
                tile = tile.astype(jnp.bfloat16)
                for i in range(groups // 2):
                    at = i * rows
                    for order, out in zip(orders, outs):
                        index = 0
                        for axis, bit in order:
                            if axis == "dp":
                                index = index * 2 + lax.rem(owner // (1 << bit), 2)
                            else:
                                index = index * 2 + ((i >> (bit - 1)) & 1)
                        count = out.shape[1]
                        out[index, :, j * 128 : (j + 1) * 128] = tile[at : at + count]
                        at += count
            return carry

        lax.fori_loop(0, owners // 2, body, 0)

    base, at = [], 0
    for t in range(steps):
        base.append(at)
        at += total >> (t + 1)

    def copy_of(part, c, t):
        half = total >> (t + 1)
        away = 1 - bit_of(*orders[c][t])
        source = terms[part][c] if t == 0 else got[part][c]
        start = away * half if t == 0 else base[t - 1] + away * half
        return pltpu.make_async_remote_copy(
            src_ref=source.at[pl.ds(start, half)],
            dst_ref=got[part][c].at[pl.ds(base[t], half)],
            send_sem=send_sem.at[part, c, t],
            recv_sem=recv_sem.at[part, c, t],
            device_id=partner(*orders[c][t]),
            device_id_type=MESH,
        )

    copies = [
        [[copy_of(part, c, t) for t in range(steps)] for c in range(chunks)] for part in range(2)
    ]

    def summed(part, c, t, at):
        half = total >> (t + 1)
        kept = bit_of(*orders[c][t]) * half
        source = terms[part][c] if t == 0 else got[part][c]
        offset = kept if t == 0 else base[t - 1] + kept
        here = got[part][c]
        return source[offset + at].astype(jnp.float32) + here[base[t] + at].astype(jnp.float32)

    def add(part, c, t, first_block, count):
        def body(i, carry):
            at = first_block + i
            got[part][c][base[t] + at] = summed(part, c, t, at).astype(jnp.bfloat16)
            return carry

        lax.fori_loop(0, count, body, 0)

    def advance(part, t):
        half = total >> (t + 2)
        for c in range(chunks):
            copies[part][c][t].wait_recv()
            nxt = bit_of(*orders[c][t + 1])
            add(part, c, t, (1 - nxt) * half, half)
            copies[part][c][t + 1].start()
        for c in range(chunks):
            nxt = bit_of(*orders[c][t + 1])
            add(part, c, t, nxt * half, half)

    def finish(part):
        finished = []
        for c in range(chunks):
            copies[part][c][steps - 1].wait_recv()
            finished.append(summed(part, c, steps - 1, 0))
        return jnp.concatenate(finished, axis=0)

    def tap_piece(ks):
        def piece(owner):
            here = slice(owner * narrow, (owner + 1) * narrow)
            parts = [taps[k, :, here].astype(jnp.float32) for k in ks]
            return parts[0] if len(parts) == 1 else jnp.concatenate(parts, axis=1)

        return piece

    place(left_out, wide_piece(upstream), layouts[0][1][0])
    loads[0].wait()
    wide_a[...] = jnp.dot(upstream[...], weight_out[...], preferred_element_type=jnp.float32)

    def first_rows(at):
        normal, _ = normalize(owner_input[at, :].astype(jnp.float32))
        first[at, :] = gelu_parts(normal * gain_in[...][None, :])[0].astype(jnp.bfloat16)

    looped(own_rows, 32, first_rows)
    loads[1].wait()
    hidden[...] = jnp.dot(first[...], weight_in[...], preferred_element_type=jnp.float32)

    def mid_rows(at):
        normal, scale = normalize(hidden[at, :])
        act, slope = gelu_parts(normal * gain_mid[...][None, :])
        mid[at, :] = act.astype(jnp.bfloat16)
        hidden[at, :] = normal
        mid_gain[at, :] = slope * gain_mid[...][None, :]
        mid_scale[at, :] = scale

    looped(own_rows, 32, mid_rows)
    fill_taps(mid, 1)
    pl.semaphore_wait(barrier, steps + 1)
    left_copies[1].start()
    place(left_conv, tap_piece(range(KERNEL_TAPS - 1)), layouts[0][0][0])
    left_copies[0].start()
    place(left_last, tap_piece((KERNEL_TAPS - 1,)), layouts[1][0][0])
    left_copies[2].start()
    loads[2].wait()
    conv = jnp.dot(taps[0], weight_conv[0], preferred_element_type=jnp.float32)
    for k in range(1, KERNEL_TAPS):
        conv = conv + jnp.dot(taps[k], weight_conv[k], preferred_element_type=jnp.float32)
    wide_b[...] = conv

    def out_rows(at):
        normal, scale = normalize(wide_b[at, :])
        act, slope = gelu_parts(normal * gain_out[...][None, :])
        out_act[at, :] = act.astype(jnp.bfloat16)
        cot = wide_a[at, :] * slope * gain_out[...][None, :]
        conv_cot[at, :] = pull_back(cot, normal, scale).astype(jnp.bfloat16)

    looped(own_rows, 32, out_rows)
    turn(right_conv, conv_cot)
    right_copies[0].start()
    turn(right_out, out_act)
    right_copies[1].start()
    fill_taps(conv_cot, -1)
    place(left_in, wide_piece(first), layouts[1][1][0])
    left_copies[3].start()
    side_bit = bit_of(*orders[1][0])
    sides = (
        (
            (left_conv, rights[0], layouts[0][0][0]),
            (left_out, rights[1], layouts[0][1][0]),
        ),
        (
            (left_last, rights[0], layouts[1][0][0]),
            (left_in, rights[2], layouts[1][1][0]),
        ),
    )
    left_copies[1].wait_recv()
    left_copies[0].wait_recv()
    right_copies[0].wait_recv()
    right_copies[1].wait_recv()
    multiply(0, 1 - side_bit, sides[0])
    copies[0][1][0].start()
    multiply(0, side_bit, sides[0])
    copies[0][0][0].start()
    copies[0][2][0].start()
    mid_cot = contract_cols(taps[0], weight_conv[0])
    for k in range(1, KERNEL_TAPS):
        mid_cot = mid_cot + contract_cols(taps[k], weight_conv[k])
    wide_b[...] = mid_cot

    def hidden_rows(at):
        cot = wide_b[at, :] * mid_gain[at, :]
        hidden_cot[at, :] = pull_back(cot, hidden[at, :], mid_scale[at, :]).astype(jnp.bfloat16)

    looped(own_rows, 32, hidden_rows)
    turn(right_in, hidden_cot)
    right_copies[2].start()
    halves = weight_in.shape[0] // 2
    wide_a[...] = contract_cols(hidden_cot[...], weight_in[:halves])
    left_copies[2].wait_recv()
    left_copies[3].wait_recv()
    right_copies[2].wait_recv()
    multiply(1, 1 - side_bit, sides[1])
    copies[1][1][0].start()
    multiply(1, side_bit, sides[1])
    copies[1][0][0].start()
    copies[1][2][0].start()
    wide_b[...] = contract_cols(hidden_cot[...], weight_in[halves:])

    def input_rows(start):
        piece = jnp.concatenate([wide_a[start, :], wide_b[start, :]], axis=1)
        normal, scale = normalize(owner_input[start, :].astype(jnp.float32))
        slope = gelu_parts(normal * gain_in[...][None, :])[1]
        grad = pull_back(piece * slope * gain_in[...][None, :], normal, scale)
        grad_input[start, :] = (upstream[start, :].astype(jnp.float32) + grad).astype(
            jnp.bfloat16
        )

    def late_rows(at):
        input_rows(pl.ds(pl.multiple_of(at.start + own_rows // 2, 32), 32))

    advance(0, 0)
    looped(own_rows // 2, 32, input_rows)
    advance(0, 1)
    advance(1, 0)
    looped(own_rows // 2, 32, late_rows)
    for t in range(2, steps):
        if t < steps - 1:
            advance(0, t)
        advance(1, t - 1)
    early_sum[...] = finish(0)
    late_sum[...] = finish(1)
    for copy in left_copies + right_copies:
        copy.wait_send()
    for part in range(2):
        for c in range(chunks):
            for t in range(steps):
                copies[part][c][t].wait_send()


def result_kernel(
    layouts, grad_rows, early_sum, late_sum, grad_input, grad_in, grad_conv, grad_out
):
    grad_input[...] = grad_rows[...]
    narrow, wide = grad_conv.shape[1], grad_in.shape[0]
    early, late = early_sum[...].T, late_sum[...].T
    for k in range(KERNEL_TAPS - 1):
        grad_conv[k] = early[k * narrow : (k + 1) * narrow]
    grad_conv[KERNEL_TAPS - 1] = late[:narrow]
    at = layouts[0][1][0]
    grad_out[...] = early[at : at + wide]
    at = layouts[1][1][0]
    grad_in[...] = late[at : at + wide]


def local(
    embedded,
    mask_token_embedding,
    destination,
    position,
    length,
    unmask_order,
    timestep,
    upstream,
    gain_in,
    weight_in,
    gain_mid,
    weight_conv,
    gain_out,
    weight_out,
):
    channels = embedded.shape[1]
    owners, groups = lax.axis_size("dp"), lax.axis_size("shard")
    own_rows = upstream.shape[0]
    inner = weight_in.shape[1]
    vmem = pl.BlockSpec(memory_space=pltpu.VMEM)
    bucket, bucket_pos, bucket_len = pl.pallas_call(
        functools.partial(dispatch_kernel, owners),
        out_shape=[
            jax.ShapeDtypeStruct((own_rows, channels), jnp.bfloat16),
            jax.ShapeDtypeStruct((own_rows, 1), jnp.int32),
            jax.ShapeDtypeStruct((own_rows, 1), jnp.int32),
        ],
        in_specs=[vmem] * 6,
        out_specs=[vmem] * 3,
        scratch_shapes=[
            pltpu.VMEM((owners, LMAX, channels), jnp.bfloat16),
            pltpu.VMEM((owners, LMAX, channels), jnp.bfloat16),
            pltpu.SemaphoreType.DMA((owners,)),
            pltpu.SemaphoreType.DMA((owners,)),
        ],
        compiler_params=pltpu.CompilerParams(
            collective_id=1, has_side_effects=True, vmem_limit_bytes=VMEM_LIMIT
        ),
        name="dispatch",
    )(
        destination[None, :],
        position[None, :],
        unmask_order[None, :],
        timestep[None, :],
        mask_token_embedding,
        embedded,
    )
    narrow, wide, rows = inner // owners, channels // owners, inner // groups
    layouts = part_layouts(narrow, wide)
    total = owners * groups // 2
    steps = total.bit_length() - 1
    counts = chunk_rows(rows)
    hbm = pl.BlockSpec(memory_space=pl.ANY)
    partial_results = pl.pallas_call(
        functools.partial(layer_kernel, owners, groups),
        out_shape=[jax.ShapeDtypeStruct((own_rows, channels), jnp.bfloat16)]
        + [jax.ShapeDtypeStruct((rows, width_of(layout)), jnp.float32) for layout in layouts],
        in_specs=[vmem] * 7 + [hbm] * 3,
        out_specs=[vmem] * 3,
        scratch_shapes=[
            pltpu.VMEM((total, n, width_of(layout)), jnp.bfloat16)
            for layout in layouts
            for n in counts
        ]
        + [
            pltpu.VMEM((total - 1, n, width_of(layout)), jnp.bfloat16)
            for layout in layouts
            for n in counts
        ]
        + [
            pltpu.VMEM((2, owners, own_rows, span_of(*item)), jnp.bfloat16)
            for layout in layouts
            for item in layout
        ]
        + [pltpu.VMEM((2, groups // 2, rows, own_rows), jnp.bfloat16)] * 3
        + [
            pltpu.VMEM((channels, inner), jnp.bfloat16),
            pltpu.VMEM((KERNEL_TAPS, inner, inner), jnp.bfloat16),
            pltpu.VMEM((channels, inner), jnp.bfloat16),
            pltpu.VMEM((own_rows, channels), jnp.bfloat16),
        ]
        + [pltpu.VMEM((own_rows, inner), jnp.bfloat16)] * 4
        + [pltpu.VMEM((KERNEL_TAPS, own_rows, inner), jnp.bfloat16)]
        + [
            pltpu.VMEM((own_rows, inner), jnp.float32),
            pltpu.VMEM((own_rows, inner), jnp.float32),
            pltpu.VMEM((own_rows, 1), jnp.float32),
            pltpu.VMEM((own_rows, inner), jnp.float32),
            pltpu.VMEM((own_rows, inner), jnp.float32),
        ]
        + [pltpu.VMEM((groups // 2, rows, own_rows), jnp.bfloat16)] * 3
        + [
            pltpu.SemaphoreType.DMA((2, 3, steps)),
            pltpu.SemaphoreType.DMA((2, 3, steps)),
            pltpu.SemaphoreType.DMA((3,)),
            pltpu.SemaphoreType.DMA((7,)),
            pltpu.SemaphoreType.DMA((7,)),
        ],
        compiler_params=pltpu.CompilerParams(
            collective_id=0, has_side_effects=True, vmem_limit_bytes=VMEM_LIMIT
        ),
        name="layer",
    )(
        bucket_pos,
        bucket_len,
        bucket,
        upstream,
        gain_in,
        gain_mid,
        gain_out,
        weight_in,
        jnp.transpose(weight_conv, (1, 0, 2)),
        weight_out,
    )
    grad_input, grad_in, grad_conv, grad_out = pl.pallas_call(
        functools.partial(result_kernel, layouts),
        out_shape=[
            jax.ShapeDtypeStruct((own_rows, channels), jnp.bfloat16),
            jax.ShapeDtypeStruct((wide, rows), jnp.float32),
            jax.ShapeDtypeStruct((KERNEL_TAPS, narrow, rows), jnp.float32),
            jax.ShapeDtypeStruct((wide, rows), jnp.float32),
        ],
        in_specs=[vmem] * 3,
        out_specs=[vmem] * 4,
        name="results",
    )(*partial_results)
    return grad_input, grad_in, jnp.transpose(grad_conv, (1, 0, 2)), grad_out


def solution(mesh):
    return jax.shard_map(
        local,
        mesh=mesh,
        in_specs=(
            P(("dp", "shard"), None),
            P(),
            P(("dp", "shard")),
            P(("dp", "shard")),
            P(("dp", "shard")),
            P(("dp", "shard")),
            P(("dp", "shard")),
            P(("dp", "shard"), None),
            P(),
            P(),
            P(),
            P(),
            P(),
            P(),
        ),
        out_specs=(
            P(("dp", "shard"), None),
            P("dp", "shard"),
            P("dp", None, "shard"),
            P("dp", "shard"),
        ),
        check_vma=False,
    )
```

```python
import jax
import jax.numpy as jnp
from jax import lax
from jax.experimental import pallas as pl
from jax.experimental.pallas import tpu as pltpu
import functools
from jax.sharding import PartitionSpec as P

KERNEL_TAPS = 5
DILATION_STEP = 16
LMAX = 80


EPS = 1e-05


def raw_shift(values, offset):
    if offset > 0:
        filler = jnp.zeros((offset, values.shape[1]), values.dtype)
        return jnp.concatenate([values[offset:], filler], axis=0)
    if offset < 0:
        filler = jnp.zeros((-offset, values.shape[1]), values.dtype)
        return jnp.concatenate([filler, values[:offset]], axis=0)
    return values


def contract_rows(left, right):
    return lax.dot_general(
        left, right, (((0,), (0,)), ((), ())), preferred_element_type=jnp.float32
    )


def contract_cols(left, right):
    return lax.dot_general(
        left, right, (((1,), (1,)), ((), ())), preferred_element_type=jnp.float32
    )


MESH = pl.DeviceIdType.MESH


def bit_orders(owners, groups):
    dp_bits = [("dp", i) for i in range(owners.bit_length() - 1)]
    chip_bits = [("shard", i) for i in range(1, groups.bit_length() - 1)]
    return (
        chip_bits + dp_bits,
        dp_bits[:1] + chip_bits + dp_bits[1:],
        dp_bits[1:] + chip_bits + dp_bits[:1],
    )


def chunk_rows(rows):
    unit = rows // 5
    return (2 * unit, 2 * unit, unit)


def round_up(value, multiple):
    return -(-value // multiple) * multiple


def placed(values, offset):
    low = offset // 128 * 128
    high = round_up(offset + values.shape[1], 128)
    parts = []
    if offset > low:
        parts.append(jnp.zeros((values.shape[0], offset - low), values.dtype))
    parts.append(values)
    if high > offset + values.shape[1]:
        parts.append(jnp.zeros((values.shape[0], high - offset - values.shape[1]), values.dtype))
    return low, (jnp.concatenate(parts, axis=1) if len(parts) > 1 else values)


FILL = 64.0
INV_SQRT2 = 0.7071067811865476
INV_SQRT_2PI = 0.3989422804014327
VMEM_LIMIT = 60 * 1024 * 1024
BLOCK_LIMIT = 8 * 1024 * 1024


def flipped(index, mask):
    other, bit = index, 0
    while (mask >> bit) > 0:
        if (mask >> bit) & 1:
            other = other + (1 - 2 * lax.rem(index // (1 << bit), 2)) * (1 << bit)
        bit += 1
    return other


def block_builder(owners, destination, place, order, timestep, token, embedded):
    slot = jnp.where(destination[...] < owners, destination[...] * LMAX + place[...], -1)
    hidden_slot = (order[...] < timestep[...]).astype(jnp.float32)

    def block_for(owner):
        rows = lax.broadcasted_iota(jnp.int32, (LMAX, slot.shape[1]), 0) + owner * LMAX
        pick = (rows == slot).astype(jnp.float32)
        live = jnp.sum(pick, axis=1, keepdims=True)
        masked = jnp.sum(pick * hidden_slot, axis=1, keepdims=True)
        block = jnp.dot(
            pick.astype(jnp.bfloat16), embedded[...], preferred_element_type=jnp.float32
        )
        block = jnp.where(masked > 0.5, token[...][None, :].astype(jnp.float32), block)
        return jnp.where(live > 0.5, block, FILL).astype(jnp.bfloat16)

    return block_for


def ordering(owners, own, got):
    lanes = lax.broadcasted_iota(jnp.int32, (1, owners * LMAX), 1)
    place_of = jnp.full((1, owners * LMAX), -1, jnp.int32)
    pos_of = jnp.zeros((1, owners * LMAX), jnp.float32)
    len_of = jnp.zeros((1, owners * LMAX), jnp.float32)
    start = jnp.zeros((1, 1), jnp.int32)
    for source in range(owners):
        marks = got[source, :, 0:128].astype(jnp.float32)[:, 0:1]
        count = jnp.sum((marks < FILL / 2).astype(jnp.float32), axis=0, keepdims=True)
        whole = count.astype(jnp.int32)
        inside = lanes - source * LMAX
        used = (inside >= 0) & (inside < whole)
        place_of = jnp.where(used, start + inside, place_of)
        pos_of = jnp.where(used, inside.astype(jnp.float32), pos_of)
        len_of = jnp.where(used, count, len_of)
        start = start + whole
    take = (
        lax.broadcasted_iota(jnp.int32, (own, owners * LMAX), 0) == place_of
    ).astype(jnp.float32)
    positions = jnp.sum(take * pos_of, axis=1, keepdims=True).astype(jnp.int32)
    lengths = jnp.sum(take * len_of, axis=1, keepdims=True).astype(jnp.int32)
    return take.astype(jnp.bfloat16), positions, lengths


def dispatch_kernel(
    owners,
    destination,
    position,
    order,
    timestep,
    token,
    embedded,
    bucket,
    bucket_pos,
    bucket_len,
    sent,
    got,
    send_sem,
    recv_sem,
):
    me, group = lax.axis_index("dp"), lax.axis_index("shard")
    barrier = pltpu.get_barrier_semaphore()
    for j in range(1, owners):
        pl.semaphore_signal(
            barrier, inc=1, device_id=(flipped(me, j), group), device_id_type=MESH
        )
    block_for = block_builder(owners, destination, position, order, timestep, token, embedded)
    copies = []
    for j in range(owners - 1, 0, -1):
        other = flipped(me, j)
        sent[j] = block_for(other)
        if j == owners - 1:
            pl.semaphore_wait(barrier, owners - 1)
        copy = pltpu.make_async_remote_copy(
            src_ref=sent.at[j],
            dst_ref=got.at[me],
            send_sem=send_sem.at[j],
            recv_sem=recv_sem.at[j],
            device_id=(other, group),
            device_id_type=MESH,
        )
        copy.start()
        copies.append(copy)
    got[me] = block_for(me)
    for copy in copies:
        copy.wait_recv()
    take, positions, lengths = ordering(owners, bucket.shape[0], got)
    bucket_pos[...] = positions
    bucket_len[...] = lengths
    bucket[...] = jnp.dot(
        take,
        got[...].reshape(owners * LMAX, bucket.shape[1]),
        preferred_element_type=jnp.float32,
    ).astype(jnp.bfloat16)
    for copy in copies:
        copy.wait_send()


def looped(rows, step, body):
    while rows % step:
        step //= 2

    def run(i, carry):
        body(pl.ds(pl.multiple_of(i * step, step), step))
        return carry

    lax.fori_loop(0, rows // step, run, 0)


def normalize(value):
    centred = value - jnp.mean(value, axis=-1, keepdims=True)
    scale = lax.rsqrt(jnp.mean(centred * centred, axis=-1, keepdims=True) + EPS)
    return centred * scale, scale


def gelu_parts(scaled):
    half = 0.5 * (1.0 + lax.erf(scaled * INV_SQRT2))
    slope = half + scaled * (INV_SQRT_2PI * jnp.exp(-0.5 * scaled * scaled))
    return scaled * half, slope


def pull_back(cot, normal, scale):
    inner = jnp.mean(cot * normal, axis=-1, keepdims=True)
    return scale * (cot - jnp.mean(cot, axis=-1, keepdims=True) - normal * inner)


def part_layouts(narrow, wide):
    early = KERNEL_TAPS - 1
    return (
        ((0, early * narrow), (early * narrow, wide)),
        ((0, narrow), (narrow, wide)),
    )


def span_of(offset, size):
    return round_up(offset + size, 128) - offset // 128 * 128


def width_of(layout):
    return round_up(layout[-1][0] + layout[-1][1], 128)


def layer_kernel(
    owners,
    groups,
    position,
    length,
    owner_input,
    upstream,
    gain_in,
    gain_mid,
    gain_out,
    weight_in_hbm,
    weight_conv_hbm,
    weight_out_hbm,
    grad_input,
    early_sum,
    late_sum,
    *scratch,
):
    chunks = 3
    terms = (scratch[0:3], scratch[3:6])
    got = (scratch[6:9], scratch[9:12])
    left_conv, left_out, left_last, left_in = scratch[12:16]
    right_conv, right_out, right_in = scratch[16:19]
    weight_in, weight_conv, weight_out = scratch[19:22]
    first, mid, out_act, conv_cot, hidden_cot, taps = scratch[22:28]
    hidden, mid_gain, mid_scale, wide_a, wide_b = scratch[28:33]
    right_conv_peer, right_out_peer, right_in_peer = scratch[33:36]
    send_sem, recv_sem, load_sem, factor_send, factor_recv = scratch[36:41]

    orders = bit_orders(owners, groups)
    steps = len(orders[0])
    total = 1 << steps
    me = {"dp": lax.axis_index("dp"), "shard": lax.axis_index("shard")}
    own_rows = owner_input.shape[0]
    narrow, wide = mid.shape[1] // owners, first.shape[1] // owners
    rows = right_conv.shape[2]
    layouts = part_layouts(narrow, wide)

    def bit_of(axis, bit):
        return lax.rem(me[axis] // (1 << bit), 2)

    def partner(axis, bit):
        other = me[axis] + (1 - 2 * bit_of(axis, bit)) * (1 << bit)
        return (other, me["shard"]) if axis == "dp" else (me["dp"], other)

    loads = [
        pltpu.make_async_copy(source, target, load_sem.at[i])
        for i, (source, target) in enumerate(
            (
                (weight_out_hbm, weight_out),
                (weight_in_hbm, weight_in),
                (weight_conv_hbm, weight_conv),
            )
        )
    ]
    for load in loads:
        load.start()
    barrier = pltpu.get_barrier_semaphore()
    for axis, bit in [("shard", 0)] + orders[0]:
        pl.semaphore_signal(barrier, inc=1, device_id=partner(axis, bit), device_id_type=MESH)
    core = bit_of("shard", 0)

    def to_other_core(number, source, target):
        return pltpu.make_async_remote_copy(
            src_ref=source,
            dst_ref=target,
            send_sem=factor_send.at[number],
            recv_sem=factor_recv.at[number],
            device_id=partner("shard", 0),
            device_id_type=MESH,
        )

    lefts = (left_conv, left_out, left_last, left_in)
    left_copies = [to_other_core(n, ref.at[0], ref.at[1]) for n, ref in enumerate(lefts)]
    rights = ((right_conv, right_conv_peer), (right_out, right_out_peer), (right_in, right_in_peer))
    right_copies = [
        to_other_core(4 + n, ref.at[1 - core], peer) for n, (ref, peer) in enumerate(rights)
    ]

    def turn(right, values):
        turned = values[...].T
        for g in range(groups):
            right[g % 2, g // 2] = turned[g * rows : (g + 1) * rows]

    tap_offsets = [(k - KERNEL_TAPS // 2) * DILATION_STEP for k in range(KERNEL_TAPS)]

    def fill_taps(source, sign):
        for k, base_offset in enumerate(tap_offsets):
            offset = sign * base_offset
            moved = position[...] + offset
            valid = (moved >= 0) & (moved < length[...])
            shifted = raw_shift(source[...], offset)
            taps[k] = jnp.where(valid, shifted.astype(jnp.float32), 0.0).astype(jnp.bfloat16)

    def place(left, pieces, offset):
        for owner in range(owners):
            values = pieces(owner)
            left[0, owner] = placed(values, offset)[1].astype(jnp.bfloat16)

    def wide_piece(source):
        return lambda owner: source[:, owner * wide : (owner + 1) * wide].astype(jnp.float32)

    def multiply(part, low_bit, sides):
        outs = terms[part]
        width = outs[0].shape[2]

        def body(pair, carry):
            owner = pair * 2 + low_bit
            tiles = [None] * (width // 128)
            for left, (right, peer), offset in sides:
                low = offset // 128
                picked = jnp.concatenate(
                    [
                        right[core].reshape(groups // 2 * rows, own_rows),
                        peer[...].reshape(groups // 2 * rows, own_rows),
                    ],
                    axis=1,
                )
                both = jnp.concatenate([left[0, owner], left[1, owner]], axis=0)
                term = jnp.dot(picked, both, preferred_element_type=jnp.float32)
                for j in range(left.shape[3] // 128):
                    piece = term[:, j * 128 : (j + 1) * 128]
                    held = tiles[low + j]
                    tiles[low + j] = piece if held is None else held + piece
            for j, tile in enumerate(tiles):
                tile = tile.astype(jnp.bfloat16)
                for i in range(groups // 2):
                    at = i * rows
                    for order, out in zip(orders, outs):
                        index = 0
                        for axis, bit in order:
                            if axis == "dp":
                                index = index * 2 + lax.rem(owner // (1 << bit), 2)
                            else:
                                index = index * 2 + ((i >> (bit - 1)) & 1)
                        count = out.shape[1]
                        out[index, :, j * 128 : (j + 1) * 128] = tile[at : at + count]
                        at += count
            return carry

        lax.fori_loop(0, owners // 2, body, 0)

    base, at = [], 0
    for t in range(steps):
        base.append(at)
        at += total >> (t + 1)

    def copy_of(part, c, t):
        half = total >> (t + 1)
        away = 1 - bit_of(*orders[c][t])
        source = terms[part][c] if t == 0 else got[part][c]
        start = away * half if t == 0 else base[t - 1] + away * half
        return pltpu.make_async_remote_copy(
            src_ref=source.at[pl.ds(start, half)],
            dst_ref=got[part][c].at[pl.ds(base[t], half)],
            send_sem=send_sem.at[part, c, t],
            recv_sem=recv_sem.at[part, c, t],
            device_id=partner(*orders[c][t]),
            device_id_type=MESH,
        )

    copies = [
        [[copy_of(part, c, t) for t in range(steps)] for c in range(chunks)] for part in range(2)
    ]

    def summed(part, c, t, at):
        half = total >> (t + 1)
        kept = bit_of(*orders[c][t]) * half
        source = terms[part][c] if t == 0 else got[part][c]
        offset = kept if t == 0 else base[t - 1] + kept
        here = got[part][c]
        return source[offset + at].astype(jnp.float32) + here[base[t] + at].astype(jnp.float32)

    def add(part, c, t, first_block, count):
        def body(i, carry):
            at = first_block + i
            got[part][c][base[t] + at] = summed(part, c, t, at).astype(jnp.bfloat16)
            return carry

        lax.fori_loop(0, count, body, 0)

    def advance(part, t, picked=(2, 1, 0)):
        half = total >> (t + 2)
        for c in picked:
            copies[part][c][t].wait_recv()
            nxt = bit_of(*orders[c][t + 1])
            add(part, c, t, (1 - nxt) * half, half)
            copies[part][c][t + 1].start()
            add(part, c, t, nxt * half, half)

    def finish(part):
        finished = []
        for c in range(chunks):
            copies[part][c][steps - 1].wait_recv()
            finished.append(summed(part, c, steps - 1, 0))
        return jnp.concatenate(finished, axis=0)

    def tap_piece(ks):
        def piece(owner):
            here = slice(owner * narrow, (owner + 1) * narrow)
            parts = [taps[k, :, here].astype(jnp.float32) for k in ks]
            return parts[0] if len(parts) == 1 else jnp.concatenate(parts, axis=1)

        return piece

    place(left_out, wide_piece(upstream), layouts[0][1][0])
    loads[0].wait()
    wide_a[...] = jnp.dot(upstream[...], weight_out[...], preferred_element_type=jnp.float32)

    def first_rows(at):
        normal, _ = normalize(owner_input[at, :].astype(jnp.float32))
        first[at, :] = gelu_parts(normal * gain_in[...][None, :])[0].astype(jnp.bfloat16)

    looped(own_rows, 128, first_rows)
    loads[1].wait()
    hidden[...] = jnp.dot(first[...], weight_in[...], preferred_element_type=jnp.float32)

    def mid_rows(at):
        normal, scale = normalize(hidden[at, :])
        act, slope = gelu_parts(normal * gain_mid[...][None, :])
        mid[at, :] = act.astype(jnp.bfloat16)
        hidden[at, :] = normal
        mid_gain[at, :] = slope * gain_mid[...][None, :]
        mid_scale[at, :] = scale

    looped(own_rows, 128, mid_rows)
    fill_taps(mid, 1)
    pl.semaphore_wait(barrier, steps + 1)
    left_copies[1].start()
    place(left_conv, tap_piece(range(KERNEL_TAPS - 1)), layouts[0][0][0])
    left_copies[0].start()
    place(left_last, tap_piece((KERNEL_TAPS - 1,)), layouts[1][0][0])
    left_copies[2].start()
    loads[2].wait()
    conv = jnp.dot(taps[0], weight_conv[0], preferred_element_type=jnp.float32)
    for k in range(1, KERNEL_TAPS):
        conv = conv + jnp.dot(taps[k], weight_conv[k], preferred_element_type=jnp.float32)
    wide_b[...] = conv

    def out_rows(at):
        normal, scale = normalize(wide_b[at, :])
        act, slope = gelu_parts(normal * gain_out[...][None, :])
        out_act[at, :] = act.astype(jnp.bfloat16)
        cot = wide_a[at, :] * slope * gain_out[...][None, :]
        conv_cot[at, :] = pull_back(cot, normal, scale).astype(jnp.bfloat16)

    looped(own_rows, 128, out_rows)
    turn(right_conv, conv_cot)
    right_copies[0].start()
    turn(right_out, out_act)
    right_copies[1].start()
    fill_taps(conv_cot, -1)
    place(left_in, wide_piece(first), layouts[1][1][0])
    left_copies[3].start()
    side_bit = bit_of(*orders[1][0])
    sides = (
        (
            (left_conv, rights[0], layouts[0][0][0]),
            (left_out, rights[1], layouts[0][1][0]),
        ),
        (
            (left_last, rights[0], layouts[1][0][0]),
            (left_in, rights[2], layouts[1][1][0]),
        ),
    )
    left_copies[1].wait_recv()
    left_copies[0].wait_recv()
    right_copies[0].wait_recv()
    right_copies[1].wait_recv()
    multiply(0, 1 - side_bit, sides[0])
    copies[0][1][0].start()
    multiply(0, side_bit, sides[0])
    copies[0][0][0].start()
    copies[0][2][0].start()
    mid_cot = contract_cols(taps[0], weight_conv[0])
    for k in range(1, KERNEL_TAPS):
        mid_cot = mid_cot + contract_cols(taps[k], weight_conv[k])
    wide_b[...] = mid_cot

    def hidden_rows(at):
        cot = wide_b[at, :] * mid_gain[at, :]
        hidden_cot[at, :] = pull_back(cot, hidden[at, :], mid_scale[at, :]).astype(jnp.bfloat16)

    looped(own_rows, 128, hidden_rows)
    turn(right_in, hidden_cot)
    right_copies[2].start()
    halves = weight_in.shape[0] // 2
    wide_a[...] = contract_cols(hidden_cot[...], weight_in[:halves])
    left_copies[2].wait_recv()
    left_copies[3].wait_recv()
    right_copies[2].wait_recv()
    multiply(1, 1 - side_bit, sides[1])
    copies[1][1][0].start()
    multiply(1, side_bit, sides[1])
    copies[1][0][0].start()
    copies[1][2][0].start()
    wide_b[...] = contract_cols(hidden_cot[...], weight_in[halves:])

    def input_rows(start):
        piece = jnp.concatenate([wide_a[start, :], wide_b[start, :]], axis=1)
        normal, scale = normalize(owner_input[start, :].astype(jnp.float32))
        slope = gelu_parts(normal * gain_in[...][None, :])[1]
        grad = pull_back(piece * slope * gain_in[...][None, :], normal, scale)
        grad_input[start, :] = (upstream[start, :].astype(jnp.float32) + grad).astype(
            jnp.bfloat16
        )

    quarter = own_rows // 4

    def input_quarter(n):
        def some(at):
            input_rows(pl.ds(pl.multiple_of(at.start + n * quarter, 32), 32))

        looped(quarter, 32, some)

    advance(0, 0, (2,))
    advance(0, 0, (1,))
    input_quarter(0)
    advance(0, 0, (0,))
    advance(1, 0, (2,))
    input_quarter(1)
    advance(1, 0, (1,))
    advance(0, 1, (2,))
    input_quarter(2)
    advance(1, 0, (0,))
    advance(0, 1, (0,))
    input_quarter(3)
    advance(0, 1, (1,))
    for t in range(2, steps):
        advance(1, t - 1, (2,))
        if t < steps - 1:
            advance(0, t, (2,))
        advance(1, t - 1, (0,))
        if t < steps - 1:
            advance(0, t, (0,))
        advance(1, t - 1, (1,))
        if t < steps - 1:
            advance(0, t, (1,))
    early_sum[...] = finish(0)
    late_sum[...] = finish(1)
    for copy in left_copies + right_copies:
        copy.wait_send()
    for part in range(2):
        for c in range(chunks):
            for t in range(steps):
                copies[part][c][t].wait_send()


def fused_kernel(
    owners,
    groups,
    destination,
    place,
    order,
    timestep,
    token,
    embedded,
    upstream,
    gain_in,
    gain_mid,
    gain_out,
    weight_in_hbm,
    weight_conv_hbm,
    weight_out_hbm,
    grad_input,
    early_sum,
    late_sum,
    *scratch,
):
    chunks = 3
    terms = (scratch[0:3], scratch[3:6])
    got = (scratch[6:9], scratch[9:12])
    left_conv, left_out, left_last, left_in = scratch[12:16]
    right_conv, right_out, right_in = scratch[16:19]
    weight_in, weight_conv, weight_out = scratch[19:22]
    first, mid, out_act, conv_cot, hidden_cot, taps = scratch[22:28]
    hidden, mid_gain, mid_scale, wide_a, wide_b = scratch[28:33]
    right_conv_peer, right_out_peer, right_in_peer = scratch[33:36]
    send_sem, recv_sem, load_sem, factor_send, factor_recv = scratch[36:41]
    sent, arrived, arrived_act, owner_input, taken, position, length = scratch[41:48]
    block_send, block_recv = scratch[48:50]

    orders = bit_orders(owners, groups)
    steps = len(orders[0])
    total = 1 << steps
    me = {"dp": lax.axis_index("dp"), "shard": lax.axis_index("shard")}
    own_rows = upstream.shape[0]
    narrow, wide = mid.shape[1] // owners, first.shape[1] // owners
    rows = right_conv.shape[2]
    layouts = part_layouts(narrow, wide)

    def bit_of(axis, bit):
        return lax.rem(me[axis] // (1 << bit), 2)

    def partner(axis, bit):
        other = me[axis] + (1 - 2 * bit_of(axis, bit)) * (1 << bit)
        return (other, me["shard"]) if axis == "dp" else (me["dp"], other)

    loads = [
        pltpu.make_async_copy(source, target, load_sem.at[i])
        for i, (source, target) in enumerate(
            (
                (weight_out_hbm, weight_out),
                (weight_in_hbm, weight_in),
                (weight_conv_hbm, weight_conv),
            )
        )
    ]
    for load in loads:
        load.start()
    barrier = pltpu.get_barrier_semaphore()
    near = [item for item in [("shard", 0)] + orders[0] if item[0] == "shard"]
    for axis, bit in near:
        pl.semaphore_signal(barrier, inc=1, device_id=partner(axis, bit), device_id_type=MESH)
    for j in range(1, owners):
        other = (flipped(me["dp"], j), me["shard"])
        pl.semaphore_signal(barrier, inc=1, device_id=other, device_id_type=MESH)
    blocks = block_builder(owners, destination, place, order, timestep, token, embedded)
    block_copies = {}
    half, quarter = owners // 2, owners // 4
    near_blocks = [j for j in range(2, half)] + [1]
    first_far = list(range(half, half + quarter))
    last_far = list(range(half + quarter, owners))
    send_order = list(dict.fromkeys(first_far + near_blocks + last_far))
    for j in send_order:
        other = flipped(me["dp"], j)
        sent[j] = blocks(other)
        if j == send_order[0]:
            pl.semaphore_wait(barrier, owners - 1 + len(near))
        block_copies[j] = pltpu.make_async_remote_copy(
            src_ref=sent.at[j],
            dst_ref=arrived.at[me["dp"]],
            send_sem=block_send.at[j],
            recv_sem=block_recv.at[j],
            device_id=(other, me["shard"]),
            device_id_type=MESH,
        )
        block_copies[j].start()
    arrived[me["dp"]] = blocks(me["dp"])
    core = bit_of("shard", 0)

    def to_other_core(number, source, target):
        return pltpu.make_async_remote_copy(
            src_ref=source,
            dst_ref=target,
            send_sem=factor_send.at[number],
            recv_sem=factor_recv.at[number],
            device_id=partner("shard", 0),
            device_id_type=MESH,
        )

    lefts = (left_conv, left_out, left_last, left_in)
    left_copies = [to_other_core(n, ref.at[0], ref.at[1]) for n, ref in enumerate(lefts)]
    rights = ((right_conv, right_conv_peer), (right_out, right_out_peer), (right_in, right_in_peer))
    right_copies = [
        to_other_core(4 + n, ref.at[1 - core], peer) for n, (ref, peer) in enumerate(rights)
    ]

    def turn(right, values):
        turned = values[...].T
        for g in range(groups):
            right[g % 2, g // 2] = turned[g * rows : (g + 1) * rows]

    tap_offsets = [(k - KERNEL_TAPS // 2) * DILATION_STEP for k in range(KERNEL_TAPS)]

    def fill_taps(source, sign):
        for k, base_offset in enumerate(tap_offsets):
            offset = sign * base_offset
            moved = position[...] + offset
            valid = (moved >= 0) & (moved < length[...])
            shifted = raw_shift(source[...], offset)
            taps[k] = jnp.where(valid, shifted.astype(jnp.float32), 0.0).astype(jnp.bfloat16)

    def place(left, pieces, offset):
        for owner in range(owners):
            values = pieces(owner)
            left[0, owner] = placed(values, offset)[1].astype(jnp.bfloat16)

    def wide_piece(source):
        return lambda owner: source[:, owner * wide : (owner + 1) * wide].astype(jnp.float32)

    def multiply(part, low_bit, sides):
        outs = terms[part]
        width = outs[0].shape[2]

        def body(pair, carry):
            owner = pair * 2 + low_bit
            tiles = [None] * (width // 128)
            for left, (right, peer), offset in sides:
                low = offset // 128
                picked = jnp.concatenate(
                    [
                        right[core].reshape(groups // 2 * rows, own_rows),
                        peer[...].reshape(groups // 2 * rows, own_rows),
                    ],
                    axis=1,
                )
                both = jnp.concatenate([left[0, owner], left[1, owner]], axis=0)
                term = jnp.dot(picked, both, preferred_element_type=jnp.float32)
                for j in range(left.shape[3] // 128):
                    piece = term[:, j * 128 : (j + 1) * 128]
                    held = tiles[low + j]
                    tiles[low + j] = piece if held is None else held + piece
            for j, tile in enumerate(tiles):
                tile = tile.astype(jnp.bfloat16)
                for i in range(groups // 2):
                    at = i * rows
                    for order, out in zip(orders, outs):
                        index = 0
                        for axis, bit in order:
                            if axis == "dp":
                                index = index * 2 + lax.rem(owner // (1 << bit), 2)
                            else:
                                index = index * 2 + ((i >> (bit - 1)) & 1)
                        count = out.shape[1]
                        out[index, :, j * 128 : (j + 1) * 128] = tile[at : at + count]
                        at += count
            return carry

        lax.fori_loop(0, owners // 2, body, 0)

    base, at = [], 0
    for t in range(steps):
        base.append(at)
        at += total >> (t + 1)

    def copy_of(part, c, t):
        half = total >> (t + 1)
        away = 1 - bit_of(*orders[c][t])
        source = terms[part][c] if t == 0 else got[part][c]
        start = away * half if t == 0 else base[t - 1] + away * half
        return pltpu.make_async_remote_copy(
            src_ref=source.at[pl.ds(start, half)],
            dst_ref=got[part][c].at[pl.ds(base[t], half)],
            send_sem=send_sem.at[part, c, t],
            recv_sem=recv_sem.at[part, c, t],
            device_id=partner(*orders[c][t]),
            device_id_type=MESH,
        )

    copies = [
        [[copy_of(part, c, t) for t in range(steps)] for c in range(chunks)] for part in range(2)
    ]

    def summed(part, c, t, at):
        half = total >> (t + 1)
        kept = bit_of(*orders[c][t]) * half
        source = terms[part][c] if t == 0 else got[part][c]
        offset = kept if t == 0 else base[t - 1] + kept
        here = got[part][c]
        return source[offset + at].astype(jnp.float32) + here[base[t] + at].astype(jnp.float32)

    def add(part, c, t, first_block, count):
        def body(i, carry):
            at = first_block + i
            got[part][c][base[t] + at] = summed(part, c, t, at).astype(jnp.bfloat16)
            return carry

        lax.fori_loop(0, count, body, 0)

    def advance(part, t, picked=(2, 1, 0)):
        half = total >> (t + 2)
        for c in picked:
            copies[part][c][t].wait_recv()
            nxt = bit_of(*orders[c][t + 1])
            add(part, c, t, (1 - nxt) * half, half)
            copies[part][c][t + 1].start()
            add(part, c, t, nxt * half, half)

    def finish(part):
        finished = []
        for c in range(chunks):
            copies[part][c][steps - 1].wait_recv()
            finished.append(summed(part, c, steps - 1, 0))
        return jnp.concatenate(finished, axis=0)

    def tap_piece(ks):
        def piece(owner):
            here = slice(owner * narrow, (owner + 1) * narrow)
            parts = [taps[k, :, here].astype(jnp.float32) for k in ks]
            return parts[0] if len(parts) == 1 else jnp.concatenate(parts, axis=1)

        return piece

    place(left_out, wide_piece(upstream), layouts[0][1][0])
    loads[0].wait()
    wide_a[...] = jnp.dot(upstream[...], weight_out[...], preferred_element_type=jnp.float32)

    def activate(source):
        def block_rows(at):
            normal, _ = normalize(arrived[source, at, :].astype(jnp.float32))
            act = gelu_parts(normal * gain_in[...][None, :])[0]
            arrived_act[source, at, :] = act.astype(jnp.bfloat16)

        looped(LMAX, 16, block_rows)

    activate(me["dp"])
    for j in dict.fromkeys(near_blocks + first_far + last_far):
        block_copies[j].wait_recv()
        activate(flipped(me["dp"], j))
    take, positions, lengths = ordering(owners, own_rows, arrived)
    position[...] = positions
    length[...] = lengths
    taken[...] = take
    first[...] = jnp.dot(
        take,
        arrived_act[...].reshape(owners * LMAX, first.shape[1]),
        preferred_element_type=jnp.float32,
    ).astype(jnp.bfloat16)
    loads[1].wait()
    hidden[...] = jnp.dot(first[...], weight_in[...], preferred_element_type=jnp.float32)

    def mid_rows(at):
        normal, scale = normalize(hidden[at, :])
        act, slope = gelu_parts(normal * gain_mid[...][None, :])
        mid[at, :] = act.astype(jnp.bfloat16)
        hidden[at, :] = normal
        mid_gain[at, :] = slope * gain_mid[...][None, :]
        mid_scale[at, :] = scale

    looped(own_rows, 128, mid_rows)
    fill_taps(mid, 1)
    left_copies[1].start()
    place(left_conv, tap_piece(range(KERNEL_TAPS - 1)), layouts[0][0][0])
    left_copies[0].start()
    place(left_last, tap_piece((KERNEL_TAPS - 1,)), layouts[1][0][0])
    left_copies[2].start()
    loads[2].wait()
    conv = jnp.dot(taps[0], weight_conv[0], preferred_element_type=jnp.float32)
    for k in range(1, KERNEL_TAPS):
        conv = conv + jnp.dot(taps[k], weight_conv[k], preferred_element_type=jnp.float32)
    wide_b[...] = conv

    def out_rows(at):
        normal, scale = normalize(wide_b[at, :])
        act, slope = gelu_parts(normal * gain_out[...][None, :])
        out_act[at, :] = act.astype(jnp.bfloat16)
        cot = wide_a[at, :] * slope * gain_out[...][None, :]
        conv_cot[at, :] = pull_back(cot, normal, scale).astype(jnp.bfloat16)

    looped(own_rows, 128, out_rows)
    turn(right_conv, conv_cot)
    right_copies[0].start()
    turn(right_out, out_act)
    right_copies[1].start()
    fill_taps(conv_cot, -1)
    place(left_in, wide_piece(first), layouts[1][1][0])
    left_copies[3].start()
    side_bit = bit_of(*orders[1][0])
    sides = (
        (
            (left_conv, rights[0], layouts[0][0][0]),
            (left_out, rights[1], layouts[0][1][0]),
        ),
        (
            (left_last, rights[0], layouts[1][0][0]),
            (left_in, rights[2], layouts[1][1][0]),
        ),
    )
    left_copies[1].wait_recv()
    left_copies[0].wait_recv()
    right_copies[0].wait_recv()
    right_copies[1].wait_recv()
    multiply(0, 1 - side_bit, sides[0])
    copies[0][1][0].start()
    multiply(0, side_bit, sides[0])
    copies[0][0][0].start()
    copies[0][2][0].start()
    mid_cot = contract_cols(taps[0], weight_conv[0])
    for k in range(1, KERNEL_TAPS):
        mid_cot = mid_cot + contract_cols(taps[k], weight_conv[k])
    wide_b[...] = mid_cot

    def hidden_rows(at):
        cot = wide_b[at, :] * mid_gain[at, :]
        hidden_cot[at, :] = pull_back(cot, hidden[at, :], mid_scale[at, :]).astype(jnp.bfloat16)

    looped(own_rows, 128, hidden_rows)
    turn(right_in, hidden_cot)
    right_copies[2].start()
    halves = weight_in.shape[0] // 2
    wide_a[...] = contract_cols(hidden_cot[...], weight_in[:halves])
    left_copies[2].wait_recv()
    left_copies[3].wait_recv()
    right_copies[2].wait_recv()
    multiply(1, 1 - side_bit, sides[1])
    copies[1][1][0].start()
    multiply(1, side_bit, sides[1])
    copies[1][0][0].start()
    copies[1][2][0].start()
    wide_b[...] = contract_cols(hidden_cot[...], weight_in[halves:])

    def input_rows(start):
        piece = jnp.concatenate([wide_a[start, :], wide_b[start, :]], axis=1)
        normal, scale = normalize(owner_input[start, :].astype(jnp.float32))
        slope = gelu_parts(normal * gain_in[...][None, :])[1]
        grad = pull_back(piece * slope * gain_in[...][None, :], normal, scale)
        grad_input[start, :] = (upstream[start, :].astype(jnp.float32) + grad).astype(
            jnp.bfloat16
        )

    piece_rows = own_rows // 4

    def input_quarter(n):
        def some(at):
            input_rows(pl.ds(pl.multiple_of(at.start + n * piece_rows, 32), 32))

        looped(piece_rows, 32, some)

    owner_input[...] = jnp.dot(
        taken[...],
        arrived[...].reshape(owners * LMAX, first.shape[1]),
        preferred_element_type=jnp.float32,
    ).astype(jnp.bfloat16)
    advance(0, 0, (2,))
    advance(0, 0, (1,))
    input_quarter(0)
    advance(0, 0, (0,))
    advance(1, 0, (2,))
    input_quarter(1)
    advance(1, 0, (1,))
    advance(0, 1, (2,))
    input_quarter(2)
    advance(1, 0, (0,))
    advance(0, 1, (0,))
    input_quarter(3)
    advance(0, 1, (1,))
    for t in range(2, steps):
        advance(1, t - 1, (2,))
        if t < steps - 1:
            advance(0, t, (2,))
        advance(1, t - 1, (0,))
        if t < steps - 1:
            advance(0, t, (0,))
        advance(1, t - 1, (1,))
        if t < steps - 1:
            advance(0, t, (1,))
    early_sum[...] = finish(0)
    late_sum[...] = finish(1)
    for copy in list(block_copies.values()) + left_copies + right_copies:
        copy.wait_send()
    for part in range(2):
        for c in range(chunks):
            for t in range(steps):
                copies[part][c][t].wait_send()


def result_kernel(
    layouts, grad_rows, early_sum, late_sum, grad_input, grad_in, grad_conv, grad_out
):
    grad_input[...] = grad_rows[...]
    narrow, wide = grad_conv.shape[1], grad_in.shape[0]
    early, late = early_sum[...].T, late_sum[...].T
    for k in range(KERNEL_TAPS - 1):
        grad_conv[k] = early[k * narrow : (k + 1) * narrow]
    grad_conv[KERNEL_TAPS - 1] = late[:narrow]
    at = layouts[0][1][0]
    grad_out[...] = early[at : at + wide]
    at = layouts[1][1][0]
    grad_in[...] = late[at : at + wide]


def local(
    embedded,
    mask_token_embedding,
    destination,
    position,
    length,
    unmask_order,
    timestep,
    upstream,
    gain_in,
    weight_in,
    gain_mid,
    weight_conv,
    gain_out,
    weight_out,
):
    channels = embedded.shape[1]
    owners, groups = lax.axis_size("dp"), lax.axis_size("shard")
    own_rows = upstream.shape[0]
    inner = weight_in.shape[1]
    vmem = pl.BlockSpec(memory_space=pltpu.VMEM)
    narrow, wide, rows = inner // owners, channels // owners, inner // groups
    layouts = part_layouts(narrow, wide)
    total = owners * groups // 2
    steps = total.bit_length() - 1
    counts = chunk_rows(rows)
    hbm = pl.BlockSpec(memory_space=pl.ANY)
    weights = (weight_in, jnp.transpose(weight_conv, (1, 0, 2)), weight_out)
    results = [jax.ShapeDtypeStruct((own_rows, channels), jnp.bfloat16)] + [
        jax.ShapeDtypeStruct((rows, width_of(layout)), jnp.float32) for layout in layouts
    ]
    scratch = (
        [
            pltpu.VMEM((total, n, width_of(layout)), jnp.bfloat16)
            for layout in layouts
            for n in counts
        ]
        + [
            pltpu.VMEM((total - 1, n, width_of(layout)), jnp.bfloat16)
            for layout in layouts
            for n in counts
        ]
        + [
            pltpu.VMEM((2, owners, own_rows, span_of(*item)), jnp.bfloat16)
            for layout in layouts
            for item in layout
        ]
        + [pltpu.VMEM((2, groups // 2, rows, own_rows), jnp.bfloat16)] * 3
        + [
            pltpu.VMEM((channels, inner), jnp.bfloat16),
            pltpu.VMEM((KERNEL_TAPS, inner, inner), jnp.bfloat16),
            pltpu.VMEM((channels, inner), jnp.bfloat16),
            pltpu.VMEM((own_rows, channels), jnp.bfloat16),
        ]
        + [pltpu.VMEM((own_rows, inner), jnp.bfloat16)] * 4
        + [pltpu.VMEM((KERNEL_TAPS, own_rows, inner), jnp.bfloat16)]
        + [
            pltpu.VMEM((own_rows, inner), jnp.float32),
            pltpu.VMEM((own_rows, inner), jnp.float32),
            pltpu.VMEM((own_rows, 1), jnp.float32),
            pltpu.VMEM((own_rows, inner), jnp.float32),
            pltpu.VMEM((own_rows, inner), jnp.float32),
        ]
        + [pltpu.VMEM((groups // 2, rows, own_rows), jnp.bfloat16)] * 3
        + [
            pltpu.SemaphoreType.DMA((2, 3, steps)),
            pltpu.SemaphoreType.DMA((2, 3, steps)),
            pltpu.SemaphoreType.DMA((3,)),
            pltpu.SemaphoreType.DMA((7,)),
            pltpu.SemaphoreType.DMA((7,)),
        ]
    )
    block_bytes = 2 * owners * LMAX * channels
    if 3 * block_bytes <= BLOCK_LIMIT:
        partial_results = pl.pallas_call(
            functools.partial(fused_kernel, owners, groups),
            out_shape=results,
            in_specs=[vmem] * 10 + [hbm] * 3,
            out_specs=[vmem] * 3,
            scratch_shapes=scratch
            + [pltpu.VMEM((owners, LMAX, channels), jnp.bfloat16)] * 3
            + [
                pltpu.VMEM((own_rows, channels), jnp.bfloat16),
                pltpu.VMEM((own_rows, owners * LMAX), jnp.bfloat16),
                pltpu.VMEM((own_rows, 1), jnp.int32),
                pltpu.VMEM((own_rows, 1), jnp.int32),
                pltpu.SemaphoreType.DMA((owners,)),
                pltpu.SemaphoreType.DMA((owners,)),
            ],
            compiler_params=pltpu.CompilerParams(
                collective_id=0, has_side_effects=True, vmem_limit_bytes=VMEM_LIMIT
            ),
            name="layer",
        )(
            destination[None, :],
            position[None, :],
            unmask_order[None, :],
            timestep[None, :],
            mask_token_embedding,
            embedded,
            upstream,
            gain_in,
            gain_mid,
            gain_out,
            *weights,
        )
    else:
        bucket, bucket_pos, bucket_len = pl.pallas_call(
            functools.partial(dispatch_kernel, owners),
            out_shape=[
                jax.ShapeDtypeStruct((own_rows, channels), jnp.bfloat16),
                jax.ShapeDtypeStruct((own_rows, 1), jnp.int32),
                jax.ShapeDtypeStruct((own_rows, 1), jnp.int32),
            ],
            in_specs=[vmem] * 6,
            out_specs=[vmem] * 3,
            scratch_shapes=[
                pltpu.VMEM((owners, LMAX, channels), jnp.bfloat16),
                pltpu.VMEM((owners, LMAX, channels), jnp.bfloat16),
                pltpu.SemaphoreType.DMA((owners,)),
                pltpu.SemaphoreType.DMA((owners,)),
            ],
            compiler_params=pltpu.CompilerParams(
                collective_id=1, has_side_effects=True, vmem_limit_bytes=VMEM_LIMIT
            ),
            name="dispatch",
        )(
            destination[None, :],
            position[None, :],
            unmask_order[None, :],
            timestep[None, :],
            mask_token_embedding,
            embedded,
        )
        partial_results = pl.pallas_call(
            functools.partial(layer_kernel, owners, groups),
            out_shape=results,
            in_specs=[vmem] * 7 + [hbm] * 3,
            out_specs=[vmem] * 3,
            scratch_shapes=scratch,
            compiler_params=pltpu.CompilerParams(
                collective_id=0, has_side_effects=True, vmem_limit_bytes=VMEM_LIMIT
            ),
            name="layer",
        )(
            bucket_pos, bucket_len, bucket, upstream, gain_in, gain_mid, gain_out, *weights
        )
    grad_input, grad_in, grad_conv, grad_out = pl.pallas_call(
        functools.partial(result_kernel, layouts),
        out_shape=[
            jax.ShapeDtypeStruct((own_rows, channels), jnp.bfloat16),
            jax.ShapeDtypeStruct((wide, rows), jnp.float32),
            jax.ShapeDtypeStruct((KERNEL_TAPS, narrow, rows), jnp.float32),
            jax.ShapeDtypeStruct((wide, rows), jnp.float32),
        ],
        in_specs=[vmem] * 3,
        out_specs=[vmem] * 4,
        name="results",
    )(*partial_results)
    return grad_input, grad_in, jnp.transpose(grad_conv, (1, 0, 2)), grad_out


def solution(mesh):
    return jax.shard_map(
        local,
        mesh=mesh,
        in_specs=(
            P(("dp", "shard"), None),
            P(),
            P(("dp", "shard")),
            P(("dp", "shard")),
            P(("dp", "shard")),
            P(("dp", "shard")),
            P(("dp", "shard")),
            P(("dp", "shard"), None),
            P(),
            P(),
            P(),
            P(),
            P(),
            P(),
        ),
        out_specs=(
            P(("dp", "shard"), None),
            P("dp", "shard"),
            P("dp", None, "shard"),
            P("dp", "shard"),
        ),
        check_vma=False,
    )
```
